32 devices in a mesh: dp: 8 (over z, y), mp: 4 (over x, core).
Axes of the slice: x: 2, y: 2, z: 4, core: 2. Of those that a mesh axis runs over, the one named last changes fastest.
Arguments:
- tokens: bfloat16 [8192, 2048], P('dp'), may hold values from -6 to 6
- out_cot: bfloat16 [8192, 2048], P('dp'), may hold values from -23 to 23
- lengths: int32 [8], P('dp'), may hold values from 1 to 1024, 6144 in all
- seq_family: int32 [8, 1], P('dp'), may hold values from 0 to 3
- family_tokens: int32 [4], replicated, may hold values from 100000 to 3999999
- norm_master: float32 [2048, 6], P('dp'), may hold values from -0.5 to 2.4, as said below
- attn_bias_master: float32 [2, 2048], P(None, 'mp'), may hold values from -2 to 2
- qkv_master: float32 [2048, 3, 2048], P('dp', None, 'mp'), may hold values from -0.125 to 0.125
- proj_master: float32 [2048, 2048], P('dp', 'mp'), may hold values from -1.5 to 1.5
- fc_bias_master: float32 [8192], P('mp'), may hold values from -1.5 to 1.5
- fc_master: float32 [2048, 8192], P('dp', 'mp'), may hold values from -0.125 to 0.125
- down_master: float32 [2048, 8192], P('dp', 'mp'), may hold values from -0.0625 to 0.0625
- norm_moment: float32 [2048, 6], P('dp'), may hold values from -0.0008544922 to 0.0008544922
- attn_bias_moment: float32 [2, 2048], P(None, 'mp'), may hold values from -0.0008544922 to 0.0008544922
- qkv_moment: float32 [2048, 3, 2048], P('dp', None, 'mp'), may hold values from -0.0008544922 to 0.0008544922
- proj_moment: float32 [2048, 2048], P('dp', 'mp'), may hold values from -0.0008544922 to 0.0008544922
- fc_bias_moment: float32 [8192], P('mp'), may hold values from -0.0008544922 to 0.0008544922
- fc_moment: float32 [2048, 8192], P('dp', 'mp'), may hold values from -0.0008544922 to 0.0008544922
- down_moment: float32 [2048, 8192], P('dp', 'mp'), may hold values from -0.0008544922 to 0.0008544922
- norm_average: float32 [2048, 6], P('dp'), may hold values from 0.5 to 1.5
- attn_bias_average: float32 [2, 2048], P(None, 'mp'), may hold values from -2 to 2
- qkv_average: float32 [2048, 3, 2048], P('dp', None, 'mp'), may hold values from -0.125 to 0.125
- proj_average: float32 [2048, 2048], P('dp', 'mp'), may hold values from -1.5 to 1.5
- fc_bias_average: float32 [8192], P('mp'), may hold values from -1.5 to 1.5
- fc_average: float32 [2048, 8192], P('dp', 'mp'), may hold values from -0.125 to 0.125
- down_average: float32 [2048, 8192], P('dp', 'mp'), may hold values from -0.0625 to 0.0625
Outputs:
- block_out: bfloat16 [8192, 2048], P('dp')
- input_grad: float32 [8192, 2048], P('dp')
- norm_grad: float32 [2048, 6], P('dp')
- attn_bias_grad: float32 [2, 2048], P(None, 'mp')
- qkv_grad: float32 [2048, 3, 2048], P('dp', None, 'mp')
- proj_grad: float32 [2048, 2048], P('dp', 'mp')
- fc_bias_grad: float32 [8192], P('mp')
- fc_grad: float32 [2048, 8192], P('dp', 'mp')
- down_grad: float32 [2048, 8192], P('dp', 'mp')
- norm_momentum: float32 [2048, 6], P('dp')
- attn_bias_momentum: float32 [2, 2048], P(None, 'mp')
- qkv_momentum: float32 [2048, 3, 2048], P('dp', None, 'mp')
- proj_momentum: float32 [2048, 2048], P('dp', 'mp')
- fc_bias_momentum: float32 [8192], P('mp')
- fc_momentum: float32 [2048, 8192], P('dp', 'mp')
- down_momentum: float32 [2048, 8192], P('dp', 'mp')
- norm_averaged: float32 [2048, 6], P('dp')
- attn_bias_averaged: float32 [2, 2048], P(None, 'mp')
- qkv_averaged: float32 [2048, 3, 2048], P('dp', None, 'mp')
- proj_averaged: float32 [2048, 2048], P('dp', 'mp')
- fc_bias_averaged: float32 [8192], P('mp')
- fc_averaged: float32 [2048, 8192], P('dp', 'mp')
- down_averaged: float32 [2048, 8192], P('dp', 'mp')
- norm_updated: float32 [2048, 6], P('dp')
- attn_bias_updated: float32 [2, 2048], P(None, 'mp')
- qkv_updated: float32 [2048, 3, 2048], P('dp', None, 'mp')
- proj_updated: float32 [2048, 2048], P('dp', 'mp')
- fc_bias_updated: float32 [8192], P('mp')
- fc_updated: float32 [2048, 8192], P('dp', 'mp')
- down_updated: float32 [2048, 8192], P('dp', 'mp')
- norm_copy: bfloat16 [2048, 6], P('dp')
- attn_bias_copy: bfloat16 [2, 2048], P(None, 'mp')
- qkv_copy: bfloat16 [2048, 3, 2048], P('dp', None, 'mp')
- proj_copy: bfloat16 [2048, 2048], P('dp', 'mp')
- fc_bias_copy: bfloat16 [8192], P('mp')
- fc_copy: bfloat16 [2048, 8192], P('dp', 'mp')
- down_copy: bfloat16 [2048, 8192], P('dp', 'mp')
- grad_norm: float32 [], replicated
The draws below stay inside these ranges and needn't reach their ends.
Inputs may be any that keep to these rules, and one draw needn't show every extreme that they name: `lengths`: they sum to 6144; the longest is 1024. `seq_family`: every family has a sequence. `norm_master`: gains positive, biases of either sign.
All inputs are finite; a program needn't handle non-finite values. No bound on the sum of `lengths` on one device may be relied on, other than what follows from the above.
Results may differ from the reference program's by a relative error of at most 0.012.
The reference program's roundings to bfloat16 on the way count: a program that leaves them out, or rounds other values in their place, can miss the bound.
Values may be sent and summed in bfloat16 or wider, within the bound.
A program may use at most 256 MiB of HBM per device.

```python
import math
import jax
import jax.numpy as jnp
import numpy as np
from jax import lax

D = 2048
HEADS = 16
HEAD_DIM = 128
FF = 8192
LEN = 1024
FAMILIES = 4
SEQS = 8
TOKENS = 8192
VALID = 6144


def draw_out_cot(key, part):
    first, second, third = jax.random.split(jax.random.fold_in(key, 11), 3)
    column = jnp.arange(D, dtype=jnp.float32) / D
    column_scale = jnp.exp(jnp.log(4.0) * (column - 0.5) + jax.random.uniform(second, (D,), jnp.float32, -0.35, 0.35))
    row_scale = jnp.exp(jax.random.uniform(third, (TOKENS, 1), jnp.float32, -0.7, 0.7))
    base = jnp.clip(jax.random.normal(first, (TOKENS, D), jnp.float32), -4.0, 4.0)
    return (base * row_scale * column_scale[None, :]).astype(jnp.bfloat16)


def draw_norm_master(key, part):
    first, second = jax.random.split(jax.random.fold_in(key, 23), 2)
    column = jnp.arange(D, dtype=jnp.float32)[:, None] / D
    gains = jnp.exp(jnp.log(3.0) * (column - 0.5) + jax.random.uniform(first, (D, 2), jnp.float32, -0.3, 0.3))
    shifts = jax.random.uniform(second, (D, 4), jnp.float32, -0.5, 0.5)
    return jnp.stack([gains[:, 0], shifts[:, 0], gains[:, 1], shifts[:, 1], shifts[:, 2], shifts[:, 3]], axis=1).astype(jnp.float32)


def touch_ends(values, key, least, largest):
    spot = [jax.random.randint(jax.random.fold_in(key, axis), (), 0, length) for axis, length in enumerate(values.shape)]
    main_axis = values.shape.index(max(values.shape))
    beside = spot[:main_axis] + [(spot[main_axis] + 1) % values.shape[main_axis]] + spot[main_axis + 1:]
    return values.at[tuple(spot)].set(least).at[tuple(beside)].set(largest)


def block_levels(rng, shape, pieces, low, largest):
    level = 1.0
    for dim, shards_of in pieces:
        draws = jax.random.uniform(jax.random.fold_in(jax.random.fold_in(rng, 6), dim), (shards_of,), jnp.float32, low / len(pieces), largest / len(pieces))
        level = level * jnp.repeat(jnp.exp(draws), shape[dim] // shards_of).reshape((-1,) + (1,) * (len(shape) - 1 - dim))
    return level


def choose_distinct(rng, rows, count, top, lift):
    order = jax.random.permutation(jax.random.fold_in(rng, 1), count)
    favour = order
    for power in range(3):
        favour = favour * favour // count
    favour = favour * lift // count
    tickets = jax.random.randint(jax.random.fold_in(rng, 2), (rows, count), 0, 4096) + favour
    holders = jax.random.permutation(jax.random.fold_in(rng, 3), rows)[jnp.arange(count) % rows]
    tickets = jnp.where(jnp.arange(rows)[:, None] == holders[None, :], 1 << 14, tickets)
    priority = tickets * count + jnp.arange(count)
    return lax.top_k(priority.astype(jnp.int32), top)[1].astype(jnp.int32)


def length_profile(amount, total, bound, skew):
    weights = [(1 << 20) // math.isqrt(rank ** skew) + 1 for rank in range(2, amount + 1)]
    spare, holding = total - bound - (amount - 1), [1] * (amount - 1)
    while spare > 0:
        candidates = [i for i in range(amount - 1) if holding[i] < bound]
        pool, remaining = sum([weights[i] for i in candidates]), spare
        for i in candidates:
            addition = min(bound - holding[i], max(1, remaining * weights[i] // pool), spare)
            holding[i] = holding[i] + addition
            spare = spare - addition
    return np.array([bound] + holding)


def uneven_parts(key, count, total, reach, lean):
    if count == 2:
        one = jax.random.randint(key, (), max(1, total - reach), min(reach, total - 1) + 1)
        return jnp.stack([one, total - one])
    sizes = jnp.asarray(length_profile(count, total, reach, lean), jnp.int32)
    pairs = (count - 1) // 2
    donor, sink = sizes[1:1 + 2 * pairs:2], sizes[2:2 + 2 * pairs:2]
    slack = jnp.minimum(donor - 1, reach - sink)
    passed = jax.random.randint(jax.random.fold_in(key, 1), (pairs,), 0, 1 << 20) % (slack + 1)
    sizes = sizes.at[1:1 + 2 * pairs:2].set(donor - passed).at[2:2 + 2 * pairs:2].set(sink + passed)
    return sizes[jax.random.permutation(jax.random.fold_in(key, 2), count)]


def gaussian(rng, dims, deviation, most, shards=(), kind=jnp.bfloat16):
    entries = deviation * jax.random.normal(rng, dims, jnp.float32)
    if shards:
        entries = entries * block_levels(rng, dims, shards, -0.22, 0.18)
    return jnp.clip(entries, -most, most).astype(kind)


def setup_inputs(seed: int = 0) -> dict:
    keys = jax.random.split(jax.random.key(seed), 27)
    tokens = gaussian(keys[0], (TOKENS, D), 1.0, 6.0, ((0, 8),))
    out_cot = draw_out_cot(jax.random.fold_in(keys[26], 71), 0)
    lengths = uneven_parts(keys[2], SEQS, VALID, LEN, 2).astype(jnp.int32)
    seq_family = choose_distinct(keys[3], SEQS, FAMILIES, 1, 4096)
    family_tokens = touch_ends(jax.random.randint(keys[4], (FAMILIES,), 100000, 4000000), jax.random.fold_in(keys[4], 1), 100000, 3999999).astype(jnp.int32)
    norm_master = draw_norm_master(jax.random.fold_in(keys[26], 71), 0)
    attn_bias_master = gaussian(keys[6], (2, D), 0.3, 2.0, ((1, 4),), jnp.float32)
    qkv_master = gaussian(keys[7], (D, 3, D), D ** -0.5, 0.125, ((0, 8), (2, 4)), jnp.float32)
    proj_master = gaussian(keys[8], (D, D), (D * 8 // LEN) ** -0.5, 1.5, ((0, 8), (1, 4)), jnp.float32)
    fc_bias_master = gaussian(keys[9], (FF,), 0.2, 1.5, ((0, 4),), jnp.float32)
    fc_master = gaussian(keys[10], (D, FF), D ** -0.5, 0.125, ((0, 8), (1, 4)), jnp.float32)
    down_master = gaussian(keys[11], (D, FF), FF ** -0.5, 0.0625, ((0, 8), (1, 4)), jnp.float32)
    norm_moment = gaussian(keys[12], (D, 6), (4 * D * D + 2 * D * FF) ** -0.5, 0.0008544922, ((0, 8),), jnp.float32)
    attn_bias_moment = gaussian(keys[13], (2, D), (4 * D * D + 2 * D * FF) ** -0.5, 0.0008544922, ((1, 4),), jnp.float32)
    qkv_moment = gaussian(keys[14], (D, 3, D), (4 * D * D + 2 * D * FF) ** -0.5, 0.0008544922, ((0, 8), (2, 4)), jnp.float32)
    proj_moment = gaussian(keys[15], (D, D), (4 * D * D + 2 * D * FF) ** -0.5, 0.0008544922, ((0, 8), (1, 4)), jnp.float32)
    fc_bias_moment = gaussian(keys[16], (FF,), (4 * D * D + 2 * D * FF) ** -0.5, 0.0008544922, ((0, 4),), jnp.float32)
    fc_moment = gaussian(keys[17], (D, FF), (4 * D * D + 2 * D * FF) ** -0.5, 0.0008544922, ((0, 8), (1, 4)), jnp.float32)
    down_moment = gaussian(keys[18], (D, FF), (4 * D * D + 2 * D * FF) ** -0.5, 0.0008544922, ((0, 8), (1, 4)), jnp.float32)
    norm_average = jnp.clip(1.0 + 0.1 * jax.random.normal(keys[19], (D, 6), jnp.float32), 0.5, 1.5)
    attn_bias_average = gaussian(keys[20], (2, D), 0.3, 2.0, ((1, 4),), jnp.float32)
    qkv_average = gaussian(keys[21], (D, 3, D), D ** -0.5, 0.125, ((0, 8), (2, 4)), jnp.float32)
    proj_average = gaussian(keys[22], (D, D), (D * 8 // LEN) ** -0.5, 1.5, ((0, 8), (1, 4)), jnp.float32)
    fc_bias_average = gaussian(keys[23], (FF,), 0.2, 1.5, ((0, 4),), jnp.float32)
    fc_average = gaussian(keys[24], (D, FF), D ** -0.5, 0.125, ((0, 8), (1, 4)), jnp.float32)
    down_average = gaussian(keys[25], (D, FF), FF ** -0.5, 0.0625, ((0, 8), (1, 4)), jnp.float32)
    return dict(tokens=tokens, out_cot=out_cot, lengths=lengths, seq_family=seq_family, family_tokens=family_tokens, norm_master=norm_master, attn_bias_master=attn_bias_master, qkv_master=qkv_master, proj_master=proj_master, fc_bias_master=fc_bias_master, fc_master=fc_master, down_master=down_master, norm_moment=norm_moment, attn_bias_moment=attn_bias_moment, qkv_moment=qkv_moment, proj_moment=proj_moment, fc_bias_moment=fc_bias_moment, fc_moment=fc_moment, down_moment=down_moment, norm_average=norm_average, attn_bias_average=attn_bias_average, qkv_average=qkv_average, proj_average=proj_average, fc_bias_average=fc_bias_average, fc_average=fc_average, down_average=down_average)


EPS = 1e-05
MOMENTUM = 0.9
RATE = 192.0
KEEP = 0.9
NEG = -1e+30
PRECISE = lax.Precision.HIGHEST

@jax.custom_vjp
def low(v):
    return lax.optimization_barrier(v.astype(jnp.bfloat16)).astype(jnp.float32)

@jax.custom_vjp
def low_back(v):
    return v

def low_keep(v):
    return (low(v), None)

def low_pass(kept, grad):
    return (grad,)

def back_keep(v):
    return (v, None)

def back_low(kept, grad):
    return (low(grad),)
low.defvjp(low_keep, low_pass)
low_back.defvjp(back_keep, back_low)

def layer_norm(value, gain, shift):
    centre = lax.optimization_barrier(jnp.mean(value, axis=-1, keepdims=True))
    centred = value - centre
    spread = lax.optimization_barrier(jnp.mean(centred * centred, axis=-1, keepdims=True))
    return centred * lax.rsqrt(spread + EPS) * gain + shift

def gelu_tanh(value):
    return 0.5 * value * (1.0 + jnp.tanh(0.7978845608028654 * (value + 0.044715 * value * value * value)))

def forward(inputs, norm_w, attn_b, qkv_w, proj_w, fc_b, fc_w, down_w):
    norm_w = low(norm_w)
    qkv_w = low(qkv_w)
    proj_w = low(proj_w)
    fc_w = low(fc_w)
    down_w = low(down_w)
    seq_len = inputs.shape[0]
    bias_rows = jnp.stack([attn_b[0], jnp.zeros_like(attn_b[0]), attn_b[1]], axis=0)
    ln1_out = low(layer_norm(inputs, norm_w[:, 0], norm_w[:, 1]))
    qkv = jnp.einsum('td,dce->tce', ln1_out, qkv_w, precision=PRECISE) + bias_rows[None]
    qkv = low_back(low(qkv))
    heads = qkv.reshape(seq_len, 3, HEADS, HEAD_DIM)
    query_rows = heads[:, 0]
    key_rows = heads[:, 1]
    value_rows = heads[:, 2]
    scores = jnp.einsum('qhd,khd->hqk', query_rows, key_rows, precision=PRECISE) * (1.0 / math.sqrt(HEAD_DIM))
    scores = low_back(scores)
    places = jnp.arange(seq_len)
    causal = places[:, None] >= places[None, :]
    scores = jnp.where(causal[None], scores, NEG)
    attn_prob = jnp.exp(scores - jax.scipy.special.logsumexp(scores, axis=-1, keepdims=True))
    mixed = jnp.einsum('hqk,khd->qhd', low(attn_prob), value_rows, precision=PRECISE).reshape(seq_len, D)
    mixed = low_back(low(mixed))
    residual = inputs + low_back(jnp.einsum('te,de->td', mixed, proj_w, precision=PRECISE)) + norm_w[:, 4]
    ln2_out = low(layer_norm(residual, norm_w[:, 2], norm_w[:, 3]))
    pre_act = low_back(jnp.einsum('td,df->tf', ln2_out, fc_w, precision=PRECISE) + fc_b)
    hidden_act = low(gelu_tanh(pre_act))
    return residual + low_back(jnp.einsum('tf,df->td', hidden_act, down_w, precision=PRECISE)) + norm_w[:, 5]

def reference(tokens, out_cot, lengths, seq_family, family_tokens, norm_master, attn_bias_master, qkv_master, proj_master, fc_bias_master, fc_master, down_master, norm_moment, attn_bias_moment, qkv_moment, proj_moment, fc_bias_moment, fc_moment, down_moment, norm_average, attn_bias_average, qkv_average, proj_average, fc_bias_average, fc_average, down_average):
    family_ids = jnp.arange(FAMILIES, dtype=jnp.int32)
    member = seq_family[:, 0:1] == family_ids[None, :]
    counts = lax.optimization_barrier(jnp.sum(jnp.where(member, lengths[:, None], 0), axis=0)).astype(jnp.float32)
    valid_total = jnp.sum(counts)
    share = family_tokens.astype(jnp.float32) / jnp.sum(family_tokens).astype(jnp.float32)
    family_weight = share * valid_total / jnp.maximum(counts, float(LEN // 2))
    seq_weight = lax.optimization_barrier(jnp.sum(jnp.where(member, family_weight[None, :], 0.0), axis=1))
    places = jnp.arange(LEN, dtype=jnp.int32)
    token_weight = jnp.where(places[None, :] < lengths[:, None], seq_weight[:, None], 0.0)
    inputs = tokens.astype(jnp.float32).reshape(SEQS, LEN, D)
    upstream = token_weight[:, :, None] * out_cot.astype(jnp.float32).reshape(SEQS, LEN, D)
    masters = (norm_master, attn_bias_master, qkv_master, proj_master, fc_bias_master, fc_master, down_master)

    def one_sequence(carry, item):
        seq_in, seq_up = item
        result, pullback = jax.vjp(forward, seq_in, *masters)
        grads = pullback(seq_up)
        return (tuple(jax.tree.map(jnp.add, carry, tuple(grads[1:]))), (result.astype(jnp.bfloat16), grads[0]))
    zeros = tuple((jnp.zeros_like(master) for master in masters))
    sums, (outputs, input_grads) = lax.scan(one_sequence, zeros, (inputs, upstream))
    block_out = outputs.reshape(TOKENS, D)
    input_grad = input_grads.reshape(TOKENS, D)
    raw_grads = [grad_sum / valid_total for grad_sum in sums]
    squares = sum((jnp.sum(grad_raw * grad_raw) for grad_raw in raw_grads))
    grad_norm = jnp.sqrt(squares)
    clip_factor = jnp.minimum(1.0, 1.0 / (grad_norm + 1e-06))
    moments = (norm_moment, attn_bias_moment, qkv_moment, proj_moment, fc_bias_moment, fc_moment, down_moment)
    averages = (norm_average, attn_bias_average, qkv_average, proj_average, fc_bias_average, fc_average, down_average)
    grads_out = []
    momenta_out = []
    averaged_out = []
    updated_out = []
    copies_out = []
    for master, moment, average, grad_raw in zip(masters, moments, averages, raw_grads):
        clipped = grad_raw * clip_factor
        momentum = MOMENTUM * moment + clipped
        updated = master - RATE * (clipped + MOMENTUM * momentum)
        averaged = KEEP * average + (1.0 - KEEP) * updated
        grads_out.append(clipped)
        momenta_out.append(momentum)
        averaged_out.append(averaged)
        updated_out.append(updated)
        copies_out.append(updated.astype(jnp.bfloat16))
    return (block_out, input_grad, grads_out[0], grads_out[1], grads_out[2], grads_out[3], grads_out[4], grads_out[5], grads_out[6], momenta_out[0], momenta_out[1], momenta_out[2], momenta_out[3], momenta_out[4], momenta_out[5], momenta_out[6], averaged_out[0], averaged_out[1], averaged_out[2], averaged_out[3], averaged_out[4], averaged_out[5], averaged_out[6], updated_out[0], updated_out[1], updated_out[2], updated_out[3], updated_out[4], updated_out[5], updated_out[6], copies_out[0], copies_out[1], copies_out[2], copies_out[3], copies_out[4], copies_out[5], copies_out[6], grad_norm)
```

```python
import math

import jax
import jax.numpy as jnp
from jax import lax
from jax.sharding import PartitionSpec as P

HEAD_DIM = 128
LEN = 1024


EPS = 1e-05
MOMENTUM = 0.9
RATE = 192.0
KEEP = 0.9
NEG = -1e30
BF16 = jnp.bfloat16
F32 = jnp.float32


def dot_f32(eq, left, right):
    return jnp.einsum(eq, left, right, preferred_element_type=F32)


def after(value, *gates):
    return lax.optimization_barrier((value, *gates))[0]


def swap(value, axis, flip):
    size = lax.axis_size(axis)
    return lax.ppermute(value, axis, [(i, i ^ flip) for i in range(size)])


def turn(value, steps):
    size = lax.axis_size("dp")
    outer = size // 2
    pairs = [(i, ((i // 2 + steps) % outer) * 2 + i % 2) for i in range(size)]
    return lax.ppermute(value, "dp", pairs)


def tree_sum(value, axis):
    bits = lax.axis_size(axis).bit_length() - 1
    low = 0
    while low < bits:
        span = min(3, bits - low)
        parts = [value] + [swap(value, axis, k << low) for k in range(1, 1 << span)]
        while len(parts) > 1:
            parts = [parts[i] + parts[i + 1] for i in range(0, len(parts), 2)]
        value = parts[0]
        low += span
    return value


def norm_stats(value):
    centre = jnp.mean(value, axis=-1, keepdims=True)
    centred = value - centre
    spread = jnp.mean(centred * centred, axis=-1, keepdims=True)
    inverse = lax.rsqrt(spread + EPS)
    return centred * inverse, inverse


def gelu_parts(value):
    inner = 0.7978845608028654 * (value + 0.044715 * value * value * value)
    return jnp.tanh(inner)


def gelu_tanh(value):
    return 0.5 * value * (1.0 + gelu_parts(value))


def gelu_slope(value):
    tanh = gelu_parts(value)
    rise = 0.7978845608028654 * (1.0 + 3.0 * 0.044715 * value * value)
    return 0.5 * (1.0 + tanh) + 0.5 * value * (1.0 - tanh * tanh) * rise


def local(
    tokens,
    out_cot,
    lengths,
    seq_family,
    family_tokens,
    norm_master,
    attn_bias_master,
    qkv_master,
    proj_master,
    fc_bias_master,
    fc_master,
    down_master,
    norm_moment,
    attn_bias_moment,
    qkv_moment,
    proj_moment,
    fc_bias_moment,
    fc_moment,
    down_moment,
    norm_average,
    attn_bias_average,
    qkv_average,
    proj_average,
    fc_bias_average,
    fc_average,
    down_average,
):
    seq_count = lengths.shape[0]
    row_count = tokens.shape[0]
    seq_len = row_count // seq_count
    family_count = family_tokens.shape[0]
    depth, _, head_width = qkv_master.shape
    local_heads = head_width // HEAD_DIM
    scale = 1.0 / math.sqrt(HEAD_DIM)
    mp_count = lax.axis_size("mp")
    dp_count = lax.axis_size("dp")
    outer = dp_count // 2
    place = lax.axis_index("dp")
    place_out, place_in = place // 2, place % 2
    side = lax.axis_index("mp") % 2
    half = row_count // 2

    def block_at(s, r):
        return ((place_out + (outer - r)) % outer) * 2 + (place_in + s) % 2

    def to_local(value):
        parts = [
            lax.dynamic_slice_in_dim(value, block_at(s, r) * depth, depth, 1)
            for s in range(2)
            for r in range(outer)
        ]
        return jnp.concatenate(parts, axis=1)

    def to_global(value):
        parts = []
        for b in range(dp_count):
            s = (b % 2 + place_in) % 2
            r = (place_out + outer - b // 2) % outer
            parts.append(lax.dynamic_slice_in_dim(value, (s * outer + r) * depth, depth, 1))
        return jnp.concatenate(parts, axis=1)

    def own_rows(value):
        return lax.dynamic_slice_in_dim(value, side * half, half, 0)

    def other_rows(value):
        return lax.dynamic_slice_in_dim(value, (1 - side) * half, half, 0)

    def halves_swapped(own, other):
        return jnp.where(
            side == 0,
            jnp.concatenate([own, other], axis=0),
            jnp.concatenate([other, own], axis=0),
        )

    def gather(shard, gate=None, axis=0):
        if gate is not None:
            shard = after(shard, *gate)
        near = [shard] + [turn(shard, r) for r in range(1, outer)]
        far = [swap(part, "dp", 1) for part in near]
        return jnp.concatenate(near + far, axis=axis), near[1:]

    low_norm = norm_master.astype(BF16).T
    low_qkv = qkv_master.astype(BF16).reshape(depth, 3 * head_width)
    low_proj = proj_master.astype(BF16)
    low_fc = fc_master.astype(BF16)
    low_down = down_master.astype(BF16)

    w_norm, _ = gather(low_norm, axis=1)
    w_qkv, gate_qkv = gather(low_qkv)
    w_proj, gate_proj = gather(low_proj, gate_qkv[:1])
    w_fc, gate_fc = gather(low_fc, gate_qkv)
    w_down, _ = gather(low_down, gate_fc)

    family_ids = jnp.arange(family_count, dtype=jnp.int32)
    member = seq_family == family_ids[None, :]
    local_counts = jnp.sum(jnp.where(member, lengths[:, None], 0), axis=0).astype(F32)
    counts = tree_sum(local_counts, "dp")
    valid_total = jnp.sum(counts)
    share = family_tokens.astype(F32) / jnp.sum(family_tokens).astype(F32)
    family_weight = share * valid_total / jnp.maximum(counts, float(LEN // 2))
    seq_weight = jnp.sum(jnp.where(member, family_weight[None, :], 0.0), axis=1)
    places = jnp.arange(seq_len, dtype=jnp.int32)
    token_weight = jnp.where(places[None, :] < lengths[:, None], seq_weight[:, None], 0.0).reshape(
        row_count
    )
    causal = places[:, None] >= places[None, :]

    norm_full = w_norm.astype(F32)
    gain1, shift1, gain2, shift2, bias_p, bias_d = [norm_full[i][None] for i in range(6)]
    bias_row = jnp.concatenate(
        [attn_bias_master[0], jnp.zeros_like(attn_bias_master[0]), attn_bias_master[1]], axis=0
    )
    x_low = to_local(tokens)
    cot_low = to_local(out_cot)

    x_hat, _ = norm_stats(x_low.astype(F32))
    ln1_low = (x_hat * gain1 + shift1).astype(BF16)
    qkv = (dot_f32("td,de->te", ln1_low, w_qkv) + bias_row[None]).astype(BF16)
    heads = qkv.reshape(seq_count, seq_len, 3, local_heads, HEAD_DIM)

    def attend(one_seq):
        query_rows = one_seq[:, 0]
        key_rows = one_seq[:, 1]
        value_rows = one_seq[:, 2]
        scores = dot_f32("qhd,khd->hqk", query_rows, key_rows) * scale
        scores = jnp.where(causal[None], scores, NEG)
        row_top = jnp.max(scores, axis=-1, keepdims=True)
        log_total = row_top + jnp.log(jnp.sum(jnp.exp(scores - row_top), axis=-1, keepdims=True))
        attn_prob = jnp.exp(scores - log_total).astype(BF16)
        mixed = dot_f32("hqk,khd->qhd", attn_prob, value_rows)
        return (mixed.astype(BF16), log_total)

    mixed_low, log_kept = lax.map(attend, heads)
    mixed_low = mixed_low.reshape(row_count, head_width)
    mixed_low = halves_swapped(mixed_low[:half], mixed_low[half:])

    def sum_over_mp(product, left):
        other = swap(product(left[half:]).astype(BF16), "mp", 1)
        part = (product(left[:half]) + other.astype(F32)).astype(BF16)
        flip = 2
        while flip < mp_count:
            part = part.astype(F32) + swap(part, "mp", flip).astype(F32)
            flip *= 2
            if flip < mp_count:
                part = part.astype(BF16)
        return part.astype(F32)

    x_own = own_rows(x_low).astype(F32)
    attn_out = sum_over_mp(lambda rows: dot_f32("te,de->td", rows, w_proj), mixed_low)
    residual = x_own + attn_out + bias_p
    hat2, inverse2 = norm_stats(residual)
    ln2_own = (hat2 * gain2 + shift2).astype(BF16)
    ln2_low = jnp.concatenate([ln2_own, swap(ln2_own, "mp", 1)], axis=0)
    pre_act = dot_f32("td,df->tf", ln2_low, w_fc) + fc_bias_master[None]
    hidden_low = gelu_tanh(pre_act).astype(BF16)

    weight_own, weight_other = own_rows(token_weight), other_rows(token_weight)
    upstream = weight_own[:, None] * own_rows(cot_low).astype(F32)
    upstream_other = weight_other[:, None] * other_rows(cot_low).astype(F32)
    upstream_low = jnp.concatenate([upstream, upstream_other], axis=0).astype(BF16)

    def reduce_grad(left, right, group):
        total = None
        for first in range(0, outer, group):
            count = min(group, outer - first)

            def block(s):
                start = (s * outer + first) * depth
                return dot_f32("td,tf->df", left[:, start : start + count * depth], right)

            given = swap(block(1).astype(BF16), "dp", 1)
            part = block(0) + given.astype(F32)
            for r in range(first, first + count):
                piece = part[(r - first) * depth : (r - first + 1) * depth]
                if r:
                    piece = turn(piece.astype(BF16), -r).astype(F32)
                total = piece if total is None else total + piece
        return total

    down_reduced = reduce_grad(upstream_low, hidden_low, 1)

    mlp_out = sum_over_mp(lambda rows: dot_f32("tf,df->td", rows, w_down), hidden_low)
    block_own = (residual + mlp_out + bias_d).astype(BF16)
    block_part = to_global(halves_swapped(block_own, swap(block_own, "mp", 1)))

    back_act = dot_f32("td,df->tf", upstream_low, w_down)
    back_pre = (back_act * gelu_slope(pre_act)).astype(BF16)
    fc_bias_sum = jnp.sum(back_pre, axis=0, dtype=F32)
    fc_reduced = reduce_grad(ln2_low, back_pre, 1)

    def norm_back(back, hat, inverse, gain):
        scaled = back * gain
        mean = jnp.mean(scaled, axis=-1, keepdims=True)
        slope = jnp.mean(scaled * hat, axis=-1, keepdims=True)
        return inverse * (scaled - mean - hat * slope)

    back_ln2 = sum_over_mp(lambda rows: dot_f32("tf,df->td", rows, w_fc), back_pre)
    gain2_sum = jnp.sum(back_ln2 * hat2, axis=0)
    shift2_sum = jnp.sum(back_ln2, axis=0)
    back_resid = upstream + norm_back(back_ln2, hat2, inverse2, gain2)
    ga_own = back_resid.astype(BF16)
    ga_low = jnp.concatenate([ga_own, swap(ga_own, "mp", 1)], axis=0)
    proj_reduced = reduce_grad(ga_low, mixed_low, outer)
    back_mixed = dot_f32("td,de->te", ga_low, w_proj).astype(BF16)
    back_mixed = halves_swapped(back_mixed[:half], back_mixed[half:])
    back_mixed = back_mixed.reshape(seq_count, seq_len, local_heads, HEAD_DIM)

    def attend_back(items):
        one_seq, log_total, back_seq = items
        query_rows = one_seq[:, 0]
        key_rows = one_seq[:, 1]
        value_rows = one_seq[:, 2]
        scores = dot_f32("qhd,khd->hqk", query_rows, key_rows) * scale
        scores = jnp.where(causal[None], scores, NEG)
        attn_prob = jnp.exp(scores - log_total)
        prob_low = attn_prob.astype(BF16)
        back_value = dot_f32("hqk,qhd->khd", prob_low, back_seq)
        back_prob = dot_f32("qhd,khd->hqk", back_seq, value_rows)
        back_score = attn_prob * (
            back_prob - jnp.sum(attn_prob * back_prob, axis=-1, keepdims=True)
        )
        back_score = back_score.astype(BF16)
        back_query = dot_f32("hqk,khd->qhd", back_score, key_rows) * scale
        back_key = dot_f32("hqk,qhd->khd", back_score, query_rows) * scale
        return jnp.stack([back_query, back_key, back_value], axis=1).astype(BF16)

    back_heads = lax.map(attend_back, (heads, log_kept, back_mixed))
    back_qkv = back_heads.reshape(row_count, 3 * head_width)
    attn_bias_sum = jnp.sum(back_qkv, axis=0, dtype=F32).reshape(3, head_width)[0::2]
    qkv_reduced = reduce_grad(ln1_low, back_qkv, 1)

    back_qkv_local = halves_swapped(back_qkv[:half], back_qkv[half:])
    back_ln1 = sum_over_mp(lambda rows: dot_f32("te,de->td", rows, w_qkv), back_qkv_local)
    hat1, inverse1 = norm_stats(x_own)
    gain1_sum = jnp.sum(back_ln1 * hat1, axis=0)
    shift1_sum = jnp.sum(back_ln1, axis=0)
    whole_own = back_resid + norm_back(back_ln1, hat1, inverse1, gain1)
    whole = to_global(halves_swapped(whole_own, swap(whole_own, "mp", 1)))

    norm_part = jnp.stack(
        [
            gain1_sum,
            shift1_sum,
            gain2_sum,
            shift2_sum,
            jnp.sum(back_resid, axis=0),
            jnp.sum(upstream, axis=0),
        ],
        axis=0,
    )
    norm_part = norm_part + swap(norm_part, "mp", 1)
    wide = outer * depth
    norm_part = norm_part[:, :wide] + swap(norm_part[:, wide:], "dp", 1)
    norm_reduced = norm_part[:, :depth]
    for r in range(1, outer):
        norm_reduced = norm_reduced + turn(norm_part[:, r * depth : (r + 1) * depth], -r)
    norm_reduced = norm_reduced.T

    attn_bias_reduced = tree_sum(attn_bias_sum, "dp")
    fc_bias_reduced = tree_sum(fc_bias_sum, "dp")
    qkv_reduced = qkv_reduced.reshape(depth, 3, head_width)
    raw_grads = [
        reduced / valid_total
        for reduced in (
            norm_reduced,
            attn_bias_reduced,
            qkv_reduced,
            proj_reduced,
            fc_bias_reduced,
            fc_reduced,
            down_reduced,
        )
    ]
    local_squares = jnp.sum(raw_grads[0] * raw_grads[0]) / float(mp_count)
    local_squares = local_squares + jnp.sum(raw_grads[1] * raw_grads[1]) / float(dp_count)
    local_squares = local_squares + jnp.sum(raw_grads[4] * raw_grads[4]) / float(dp_count)
    for grad_raw in (raw_grads[2], raw_grads[3], raw_grads[5], raw_grads[6]):
        local_squares = local_squares + jnp.sum(grad_raw * grad_raw)
    squares = tree_sum(tree_sum(local_squares, "mp"), "dp")
    grad_norm = jnp.sqrt(squares)
    clip_factor = jnp.minimum(1.0, 1.0 / (grad_norm + 1e-06))
    masters = (
        norm_master,
        attn_bias_master,
        qkv_master,
        proj_master,
        fc_bias_master,
        fc_master,
        down_master,
    )
    moments = (
        norm_moment,
        attn_bias_moment,
        qkv_moment,
        proj_moment,
        fc_bias_moment,
        fc_moment,
        down_moment,
    )
    averages = (
        norm_average,
        attn_bias_average,
        qkv_average,
        proj_average,
        fc_bias_average,
        fc_average,
        down_average,
    )
    grads_out = []
    momenta_out = []
    averaged_out = []
    updated_out = []
    copies_out = []
    for master, moment, average, grad_raw in zip(masters, moments, averages, raw_grads):
        clipped = grad_raw * clip_factor
        momentum = MOMENTUM * moment + clipped
        updated = master - RATE * (clipped + MOMENTUM * momentum)
        averaged = KEEP * average + (1.0 - KEEP) * updated
        grads_out.append(clipped)
        momenta_out.append(momentum)
        averaged_out.append(averaged)
        updated_out.append(updated)
        copies_out.append(updated.astype(jnp.bfloat16))
    return (
        block_part,
        whole,
        grads_out[0],
        grads_out[1],
        grads_out[2],
        grads_out[3],
        grads_out[4],
        grads_out[5],
        grads_out[6],
        momenta_out[0],
        momenta_out[1],
        momenta_out[2],
        momenta_out[3],
        momenta_out[4],
        momenta_out[5],
        momenta_out[6],
        averaged_out[0],
        averaged_out[1],
        averaged_out[2],
        averaged_out[3],
        averaged_out[4],
        averaged_out[5],
        averaged_out[6],
        updated_out[0],
        updated_out[1],
        updated_out[2],
        updated_out[3],
        updated_out[4],
        updated_out[5],
        updated_out[6],
        copies_out[0],
        copies_out[1],
        copies_out[2],
        copies_out[3],
        copies_out[4],
        copies_out[5],
        copies_out[6],
        grad_norm,
    )


def solution(mesh):
    placed = (
        P("dp", None),
        P("dp", None),
        P("dp"),
        P("dp", None),
        P(),
        P("dp", None),
        P(None, "mp"),
        P("dp", None, "mp"),
        P("dp", "mp"),
        P("mp"),
        P("dp", "mp"),
        P("dp", "mp"),
        P("dp", None),
        P(None, "mp"),
        P("dp", None, "mp"),
        P("dp", "mp"),
        P("mp"),
        P("dp", "mp"),
        P("dp", "mp"),
        P("dp", None),
        P(None, "mp"),
        P("dp", None, "mp"),
        P("dp", "mp"),
        P("mp"),
        P("dp", "mp"),
        P("dp", "mp"),
    )
    return jax.shard_map(
        local,
        mesh=mesh,
        in_specs=placed,
        out_specs=(
            P("dp", None),
            P("dp", None),
            P("dp", None),
            P(None, "mp"),
            P("dp", None, "mp"),
            P("dp", "mp"),
            P("mp"),
            P("dp", "mp"),
            P("dp", "mp"),
            P("dp", None),
            P(None, "mp"),
            P("dp", None, "mp"),
            P("dp", "mp"),
            P("mp"),
            P("dp", "mp"),
            P("dp", "mp"),
            P("dp", None),
            P(None, "mp"),
            P("dp", None, "mp"),
            P("dp", "mp"),
            P("mp"),
            P("dp", "mp"),
            P("dp", "mp"),
            P("dp", None),
            P(None, "mp"),
            P("dp", None, "mp"),
            P("dp", "mp"),
            P("mp"),
            P("dp", "mp"),
            P("dp", "mp"),
            P("dp", None),
            P(None, "mp"),
            P("dp", None, "mp"),
            P("dp", "mp"),
            P("mp"),
            P("dp", "mp"),
            P("dp", "mp"),
            P(),
        ),
        check_vma=False,
    )
```

```python
import functools
import math

import jax
import jax.numpy as jnp
from jax import lax
from jax.experimental import pallas as pl
from jax.experimental.pallas import tpu as pltpu
from jax.sharding import PartitionSpec as P

HEAD_DIM = 128
LEN = 1024


EPS = 1e-05
MOMENTUM = 0.9
RATE = 192.0
KEEP = 0.9
NEG = -1e30
BF16 = jnp.bfloat16
F32 = jnp.float32
MESH = pl.DeviceIdType.MESH


def dot_f32(eq, left, right):
    return jnp.einsum(eq, left, right, preferred_element_type=F32)


def swap(value, axis, flip):
    size = lax.axis_size(axis)
    return lax.ppermute(value, axis, [(i, i ^ flip) for i in range(size)])


def gather_kernel(outer, pieces, count, *refs):
    shards, wholes = refs[:count], refs[count : 2 * count]
    send, recv, local = refs[2 * count :]
    me = lax.axis_index("dp")
    out, side = me // 2, me % 2
    pair = out * 2 + 1 - side
    hops = outer - 1
    total = len(pieces)
    line = ((0, 1), (1, -1))

    def has(way, steps):
        return out >= steps if way > 0 else out + steps < outer

    def follows(way):
        return out + 1 < outer if way > 0 else out >= 1

    barrier = pltpu.get_barrier_semaphore()
    for peer in [lax.rem(out + r, outer) * 2 + side for r in range(1, outer)] + [pair]:
        pl.semaphore_signal(barrier, inc=1, device_id={"dp": peer}, device_id_type=MESH)
    pl.semaphore_wait(barrier, outer)

    def slot(p, device):
        a, plane, start, rows, _ = pieces[p]
        depth = shards[a].shape[-2]
        where = pl.ds(device * depth + start, rows)
        if plane is None:
            return wholes[a].at[where]
        width = shards[a].shape[-1]
        return wholes[a].at[where, pl.ds(plane * width, width)]

    def own(p):
        a, plane, start, rows, _ = pieces[p]
        where = pl.ds(start, rows)
        return shards[a].at[where] if plane is None else shards[a].at[plane, where]

    def remote(p, lane, source, target, peer):
        return pltpu.make_async_remote_copy(
            src_ref=source,
            dst_ref=target,
            send_sem=send.at[p, lane],
            recv_sem=recv.at[p, lane],
            device_id={"dp": peer},
            device_id_type=MESH,
        )

    def pass_on(p, other, index, way, steps):
        origin = (out - way * (steps - 1)) * 2 + (1 - side if other else side)
        here = slot(p, origin)
        source = own(p) if steps == 1 and not other else here
        lane = (2 * int(other) + index) * hops + steps - 1
        return remote(p, lane, source, here, (out + way) * 2 + side)

    def arrival(p, other, index, way, steps):
        origin = (out - way * steps) * 2 + (1 - side if other else side)
        lane = (2 * int(other) + index) * hops + steps - 1
        return remote(p, lane, slot(p, origin), slot(p, origin), pair)

    def to_pair(p, index, way, steps):
        if steps == 0:
            return remote(p, 4 * hops, own(p), slot(p, me), pair)
        here = slot(p, (out - way * steps) * 2 + side)
        return remote(p, (2 + index) * hops + steps - 1, here, here, pair)

    def begin(p):
        to_pair(p, 0, 1, 0).start()
        pltpu.make_async_copy(own(p), slot(p, me), local.at[p]).start()
        for index, way in line:

            @pl.when(follows(way))
            def _():
                pass_on(p, False, index, way, 1).start()

    def proceed(p, other, steps):
        early = pieces[p][4]
        for index, way in line:

            @pl.when(has(way, steps))
            def _():
                arrival(p, other, index, way, steps).wait_recv()
                if not early:
                    to_pair(p, index, way, steps).start()

            if steps < hops:

                @pl.when(jnp.logical_and(has(way, steps), follows(way)))
                def _():
                    pass_on(p, other, index, way, steps + 1).start()

    def cross(p):
        to_pair(p, 0, 1, 0).wait_recv()
        for index, way in line:

            @pl.when(follows(way))
            def _():
                pass_on(p, True, index, way, 1).start()

    lead = 4
    for p in range(min(lead, total)):
        begin(p)
    for wave in range(total + outer):
        if wave + lead < total:
            begin(wave + lead)
        if wave < total and pieces[wave][4]:
            cross(wave)
        for steps in range(1, outer):
            p = wave - steps + 1
            if 0 <= p < total:
                proceed(p, False, steps)
            p -= 1
            if 0 <= p < total and pieces[p][4]:
                proceed(p, True, steps)
    for p in range(total):
        early = pieces[p][4]
        to_pair(p, 0, 1, 0).wait_send()
        if not early:
            to_pair(p, 0, 1, 0).wait_recv()
        pltpu.make_async_copy(own(p), slot(p, me), local.at[p]).wait()
        for index, way in line:
            for other in (False, True) if early else (False,):
                for steps in range(1, outer):

                    @pl.when(jnp.logical_and(has(way, steps - 1), follows(way)))
                    def _():
                        pass_on(p, other, index, way, steps).wait_send()

            if not early:
                for steps in range(1, outer):

                    @pl.when(has(way, steps))
                    def _():
                        to_pair(p, index, way, steps).wait_send()
                        remote(
                            p,
                            (2 + index) * hops + steps - 1,
                            slot(p, me),
                            slot(p, (out - way * steps) * 2 + 1 - side),
                            pair,
                        ).wait_recv()


def gather_rows(shards, cuts, early, collective_id):
    size = lax.axis_size("dp")
    outer = size // 2
    count = len(shards)
    pieces, shapes = [], []
    for a, shard in enumerate(shards):
        depth, width = shard.shape[-2:]
        planes = [None] if shard.ndim == 2 else list(range(shard.shape[0]))
        rows = depth // cuts[a]
        for plane in planes:
            for i in range(cuts[a]):
                pieces.append((a, plane, i * rows, rows, len(pieces) in early))
        shapes.append(jax.ShapeDtypeStruct((size * depth, width * len(planes)), shard.dtype))
    anywhere = pl.BlockSpec(memory_space=pl.ANY)
    lanes = pltpu.SemaphoreType.DMA((len(pieces), 4 * outer - 3))
    return pl.pallas_call(
        functools.partial(gather_kernel, outer, pieces, count),
        out_shape=shapes,
        in_specs=[anywhere] * count,
        out_specs=[anywhere] * count,
        scratch_shapes=[lanes, lanes, pltpu.SemaphoreType.DMA((len(pieces),))],
        compiler_params=pltpu.CompilerParams(collective_id=collective_id, has_side_effects=True),
    )(*shards)


def reduce_kernel(outer, depth, cuts, count, crossings, *refs):
    refs = list(refs)

    def take(number):
        return [refs.pop(0) for _ in range(number)]

    grads, (total_ref,), crossed = take(count), take(1), take(crossings)
    raws, (square_ref,), taken = take(count), take(1), take(crossings)
    rest = refs
    own, got, given, come = [rest[i * count : (i + 1) * count] for i in range(4)]
    pair_send, pair_recv, turn_send, turn_recv, local, cross_send, cross_recv = rest[4 * count :]
    me, across = lax.axis_index("dp"), lax.axis_index("mp")
    out, side = me // 2, me % 2
    pair = out * 2 + 1 - side
    other = lax.rem(across + 2, 4)

    def member(steps):
        return lax.rem(out + steps, outer) * 2 + side

    barrier = pltpu.get_barrier_semaphore()
    for peer in [member(r) for r in range(1, outer)] + [pair]:
        pl.semaphore_signal(barrier, inc=1, device_id={"dp": peer}, device_id_type=MESH)
    pl.semaphore_signal(barrier, inc=1, device_id={"mp": other}, device_id_type=MESH)
    pl.semaphore_wait(barrier, outer + 1)

    crosses = [
        pltpu.make_async_remote_copy(
            src_ref=crossed[i],
            dst_ref=taken[i],
            send_sem=cross_send.at[i],
            recv_sem=cross_recv.at[i],
            device_id={"mp": other},
            device_id_type=MESH,
        )
        for i in range(crossings)
    ]
    for cross in crosses:
        cross.start()
    loads = [
        pltpu.make_async_copy(grads[a].at[pl.ds(0, outer * depth)], own[a], local.at[a])
        for a in range(count)
    ]
    for load in loads:
        load.start()

    pieces = []
    for a in range(count):
        rows = depth // cuts[a]
        pieces += [(a, i * rows, rows) for i in range(cuts[a])]
    order = list(range(1, outer)) + [0]

    def to_pair(p, a, start, rows, r):
        return pltpu.make_async_remote_copy(
            src_ref=grads[a].at[pl.ds((outer + r) * depth + start, rows)],
            dst_ref=got[a].at[pl.ds(r * depth + start, rows)],
            send_sem=pair_send.at[p, r],
            recv_sem=pair_recv.at[p, r],
            device_id={"dp": pair},
            device_id_type=MESH,
        )

    def to_member(p, a, start, rows, r):
        return pltpu.make_async_remote_copy(
            src_ref=given[a].at[pl.ds(r * depth + start, rows)],
            dst_ref=come[a].at[pl.ds(r * depth + start, rows)],
            send_sem=turn_send.at[p, r],
            recv_sem=turn_recv.at[p, r],
            device_id={"dp": member(outer - r)},
            device_id_type=MESH,
        )

    for p, piece in enumerate(pieces):
        for r in order:
            to_pair(p, *piece, r).start()
    for load in loads:
        load.wait()
    for p, (a, start, rows) in enumerate(pieces):
        for r in order:
            where = pl.ds(r * depth + start, rows)
            to_pair(p, a, start, rows, r).wait_recv()
            part = own[a][where].astype(F32) + got[a][where].astype(F32)
            if r:
                given[a][where] = part.astype(BF16)
                to_member(p, a, start, rows, r).start()
            else:
                raws[a][pl.ds(start, rows)] = part
    total = total_ref[0:1, 0:1]
    square = jnp.zeros((1, 1), F32)
    for p, (a, start, rows) in enumerate(pieces):
        part = raws[a][pl.ds(start, rows)]
        for r in range(1, outer):
            to_member(p, a, start, rows, r).wait_recv()
            part = part + come[a][pl.ds(r * depth + start, rows)].astype(F32)
        part = part / total
        raws[a][pl.ds(start, rows)] = part
        square = square + jnp.sum(part * part, keepdims=True)
    square_ref[...] = jnp.broadcast_to(square, square_ref.shape)
    for p, piece in enumerate(pieces):
        for r in order:
            to_pair(p, *piece, r).wait_send()
            if r:
                to_member(p, *piece, r).wait_send()
    for cross in crosses:
        cross.wait()


def reduce_rows(grads, total, crossed, cuts, collective_id):
    size = lax.axis_size("dp")
    outer = size // 2
    count, depth, number = len(grads), grads[0].shape[0] // size, sum(cuts)
    anywhere = pl.BlockSpec(memory_space=pl.ANY)
    inside = pl.BlockSpec(memory_space=pltpu.VMEM)
    buffers = [pltpu.VMEM((outer * depth, grad.shape[1]), BF16) for grad in grads]
    ways = pltpu.SemaphoreType.DMA((number, outer))
    crossings = len(crossed)
    results = pl.pallas_call(
        functools.partial(reduce_kernel, outer, depth, cuts, count, crossings),
        out_shape=[jax.ShapeDtypeStruct((depth, grad.shape[1]), F32) for grad in grads]
        + [jax.ShapeDtypeStruct((8, 128), F32)]
        + [jax.ShapeDtypeStruct(part.shape, part.dtype) for part in crossed],
        in_specs=[anywhere] * count + [inside] + [anywhere] * crossings,
        out_specs=[inside] * (count + 1) + [anywhere] * crossings,
        scratch_shapes=buffers * 4
        + [ways] * 4
        + [pltpu.SemaphoreType.DMA((count,))]
        + [pltpu.SemaphoreType.DMA((crossings,))] * 2,
        compiler_params=pltpu.CompilerParams(
            collective_id=collective_id, has_side_effects=True, vmem_limit_bytes=56 << 20
        ),
    )(*grads, total, *crossed)
    return results[:count], results[count], results[count + 1 :]


def finish_kernel(dp_count, mp_count, *refs):
    norm_ref, bias_ref, square_ref, total_ref, whole_ref = refs[:5]
    norm_out, bias_out, square_out, whole_out = refs[5:9]
    norm_in, bias_in, square_in, square_own = refs[9:13]
    norm_send, norm_recv, bias_send, bias_recv, square_send, square_recv = refs[13:19]
    whole_send, whole_recv = refs[19:21]
    me, across = lax.axis_index("dp"), lax.axis_index("mp")
    side = across % 2
    near = across + 1 - 2 * side

    def spot(kd, km):
        return {"dp": lax.rem(me + kd, dp_count), "mp": lax.rem(across + km, mp_count)}

    hops = [(kd, km) for kd in range(dp_count) for km in range(mp_count)][1:]
    barrier = pltpu.get_barrier_semaphore()
    for kd, km in hops:
        pl.semaphore_signal(barrier, inc=1, device_id=spot(kd, km), device_id_type=MESH)
    pl.semaphore_wait(barrier, len(hops))

    def send(source, target, send_sem, recv_sem, device):
        return pltpu.make_async_remote_copy(
            src_ref=source,
            dst_ref=target,
            send_sem=send_sem,
            recv_sem=recv_sem,
            device_id=device,
            device_id_type=MESH,
        )

    whole = send(whole_ref, whole_out, whole_send, whole_recv, {"mp": near})
    sent = []
    for kd in range(dp_count):
        owner = lax.rem(me + kd, dp_count)
        for flip in range(2):
            if kd or flip:
                column = near if flip else across
                copy = send(
                    norm_ref.at[owner],
                    norm_in.at[me * 2 + side],
                    norm_send.at[kd, flip],
                    norm_recv.at[kd, flip],
                    {"dp": owner, "mp": column},
                )
                copy.start()
                sent.append(copy)
    for kd in range(1, dp_count):
        copy = send(bias_ref, bias_in.at[me], bias_send.at[kd], bias_recv.at[kd], spot(kd, 0))
        copy.start()
        sent.append(copy)
    whole.start()
    norm_in[me * 2 + side] = norm_ref[me]
    bias_in[me] = bias_ref[...]
    for copy in sent:
        copy.wait_recv()
    total = total_ref[0:1, 0:1]
    norm = norm_in[0]
    for i in range(1, 2 * dp_count):
        norm = norm + norm_in[i]
    bias = bias_in[0]
    for i in range(1, dp_count):
        bias = bias + bias_in[i]
    norm = norm / total
    bias = bias / total
    norm_out[...] = norm
    bias_out[...] = bias
    square = jnp.sum(norm * norm, keepdims=True) / float(mp_count)
    square = square + jnp.sum(bias * bias, keepdims=True) / float(dp_count)
    square_own[...] = square_ref[...] + square
    slot = me * mp_count + across
    square_in[slot] = square_own[...]
    last = []
    for i, (kd, km) in enumerate(hops):
        copy = send(
            square_own, square_in.at[slot], square_send.at[i], square_recv.at[i], spot(kd, km)
        )
        copy.start()
        last.append(copy)
    for copy in last:
        copy.wait_recv()
    square = square_in[0]
    for i in range(1, dp_count * mp_count):
        square = square + square_in[i]
    square_out[...] = square
    for copy in sent + last:
        copy.wait_send()
    whole.wait()


def finish_sums(norm_part, bias_part, square, total, whole, collective_id):
    dp_count, mp_count = lax.axis_size("dp"), lax.axis_size("mp")
    anywhere = pl.BlockSpec(memory_space=pl.ANY)
    inside = pl.BlockSpec(memory_space=pltpu.VMEM)
    tile = jax.ShapeDtypeStruct((8, 128), F32)
    hops = dp_count * mp_count - 1
    return pl.pallas_call(
        functools.partial(finish_kernel, dp_count, mp_count),
        out_shape=[
            jax.ShapeDtypeStruct(norm_part.shape[1:], F32),
            jax.ShapeDtypeStruct(bias_part.shape, F32),
            tile,
            jax.ShapeDtypeStruct(whole.shape, whole.dtype),
        ],
        in_specs=[inside] * 4 + [anywhere],
        out_specs=[inside] * 3 + [anywhere],
        scratch_shapes=[
            pltpu.VMEM((2 * dp_count, *norm_part.shape[1:]), F32),
            pltpu.VMEM((dp_count, *bias_part.shape), F32),
            pltpu.VMEM((dp_count * mp_count, 8, 128), F32),
            pltpu.VMEM((8, 128), F32),
        ]
        + [pltpu.SemaphoreType.DMA((dp_count, 2))] * 2
        + [pltpu.SemaphoreType.DMA((dp_count,))] * 2
        + [pltpu.SemaphoreType.DMA((hops,))] * 2
        + [pltpu.SemaphoreType.DMA] * 2,
        compiler_params=pltpu.CompilerParams(
            collective_id=collective_id, has_side_effects=True, vmem_limit_bytes=32 << 20
        ),
    )(norm_part, bias_part, square, total, whole)


def step_kernel(count, whole_count, square_ref, total_ref, *refs):
    raws, masters, moments, averages = [refs[i * count : (i + 1) * count] for i in range(4)]
    outs = [refs[(4 + i) * count : (5 + i) * count] for i in range(5)]
    clip = jnp.minimum(1.0, 1.0 / (jnp.sqrt(square_ref[0:1, 0:1]) + 1e-06))
    total = total_ref[0:1, 0:1]

    def update(raw, master, moment, average):
        if raw.dtype == BF16:
            raw = raw.astype(F32) / total
        clipped = raw * clip
        momentum = MOMENTUM * moment + clipped
        updated = master - RATE * (clipped + MOMENTUM * momentum)
        averaged = KEEP * average + (1.0 - KEEP) * updated
        return clipped, momentum, averaged, updated, updated.astype(BF16)

    def apply(a):
        if len(masters[a].shape) == 2:
            results = update(raws[a][...], masters[a][...], moments[a][...], averages[a][...])
            for out, result in zip(outs, results):
                out[a][...] = result
        else:
            width = masters[a].shape[2]
            for c in range(masters[a].shape[0]):
                results = update(
                    raws[a][:, c * width : (c + 1) * width],
                    masters[a][c],
                    moments[a][c],
                    averages[a][c],
                )
                for out, result in zip(outs, results):
                    out[a][c] = result

    for a in range(whole_count, count):
        apply(a)

    @pl.when(pl.program_id(0) == 0)
    def _():
        for a in range(whole_count):
            apply(a)


def step_all(square, total, raws, masters, moments, averages, whole_count):
    depth = raws[-1].shape[0]
    rows = min(32, depth)

    def spec(value, a):
        shape = value.shape
        if a < whole_count:
            return pl.BlockSpec(shape, lambda i, n=len(shape): (0,) * n)
        if len(shape) == 3:
            return pl.BlockSpec((shape[0], rows, shape[2]), lambda i: (0, i, 0))
        return pl.BlockSpec((rows, shape[1]), lambda i: (i, 0))

    def specs(values):
        return [spec(value, a) for a, value in enumerate(values)]

    tile = pl.BlockSpec((8, 128), lambda i: (0, 0))
    wide = [jax.ShapeDtypeStruct(master.shape, F32) for master in masters]
    slim = [jax.ShapeDtypeStruct(master.shape, BF16) for master in masters]
    results = pl.pallas_call(
        functools.partial(step_kernel, len(masters), whole_count),
        grid=(depth // rows,),
        out_shape=wide * 4 + slim,
        in_specs=[tile, tile] + specs(raws) + specs(masters) * 3,
        out_specs=specs(masters) * 5,
        compiler_params=pltpu.CompilerParams(vmem_limit_bytes=56 << 20),
    )(square, total, *raws, *masters, *moments, *averages)
    count = len(masters)
    return [results[i * count : (i + 1) * count] for i in range(5)]


def merge_kernel(side_ref, own_ref, other_ref, out_ref):
    @pl.when(pl.program_id(0) == 0)
    def _():
        out_ref[...] = own_ref[...]

    @pl.when(pl.program_id(0) == 1)
    def _():
        out_ref[...] = other_ref[...]


def merge_halves(side, own, other):
    half, width = own.shape
    rows = min(128, half)
    steps = half // rows
    return pl.pallas_call(
        merge_kernel,
        out_shape=jax.ShapeDtypeStruct((2 * half, width), own.dtype),
        grid_spec=pltpu.PrefetchScalarGridSpec(
            num_scalar_prefetch=1,
            grid=(2, steps),
            in_specs=[
                pl.BlockSpec((rows, width), lambda h, i, side: (jnp.where(h == 0, i, steps - 1), 0)),
                pl.BlockSpec((rows, width), lambda h, i, side: (jnp.where(h == 0, 0, i), 0)),
            ],
            out_specs=pl.BlockSpec(
                (rows, width),
                lambda h, i, side: (jnp.where(h == 0, side[0], 1 - side[0]) * steps + i, 0),
            ),
        ),
    )(jnp.reshape(side, (1,)).astype(jnp.int32), own, other)


def score_block(query_ref, key_ref, first, rows, scale):
    width = first + rows
    scores = scale * lax.dot_general(
        query_ref[first:width], key_ref[:width], (((1,), (1,)), ((), ())), preferred_element_type=F32
    )
    row = first + lax.broadcasted_iota(jnp.int32, (rows, width), 0)
    column = lax.broadcasted_iota(jnp.int32, (rows, width), 1)
    scores = jnp.where(column <= row, scores, NEG)
    raised = jnp.exp(scores - jnp.max(scores, axis=-1, keepdims=True))
    return raised / jnp.sum(raised, axis=-1, keepdims=True)


def attend_kernel(rows, scale, query_ref, key_ref, value_ref, out_ref):
    for first in range(0, query_ref.shape[0], rows):
        prob = score_block(query_ref, key_ref, first, rows, scale)
        out_ref[first : first + rows] = jnp.dot(
            prob.astype(BF16), value_ref[: first + rows], preferred_element_type=F32
        ).astype(BF16)


def attend_back_kernel(
    rows, scale, query_ref, key_ref, value_ref, back_ref, gq_ref, gk_ref, gv_ref, key_sum, value_sum
):
    key_sum[...] = jnp.zeros_like(key_sum)
    value_sum[...] = jnp.zeros_like(value_sum)
    over_rows = (((0,), (0,)), ((), ()))
    for first in range(0, query_ref.shape[0], rows):
        width = first + rows
        prob = score_block(query_ref, key_ref, first, rows, scale)
        back = back_ref[first:width]
        back_prob = lax.dot_general(
            back, value_ref[:width], (((1,), (1,)), ((), ())), preferred_element_type=F32
        )
        value_sum[:width] += lax.dot_general(
            prob.astype(BF16), back, over_rows, preferred_element_type=F32
        )
        slope = jnp.sum(prob * back_prob, axis=-1, keepdims=True)
        back_score = (prob * (back_prob - slope)).astype(BF16)
        gq_ref[first:width] = (
            scale * jnp.dot(back_score, key_ref[:width], preferred_element_type=F32)
        ).astype(BF16)
        key_sum[:width] += lax.dot_general(
            back_score, query_ref[first:width], over_rows, preferred_element_type=F32
        )
    gk_ref[...] = (scale * key_sum[...]).astype(BF16)
    gv_ref[...] = value_sum[...].astype(BF16)


def attend(qkv, seq_count, heads):
    seq_len = qkv.shape[0] // seq_count
    rows = min(256, seq_len)
    columns = [
        pl.BlockSpec((seq_len, HEAD_DIM), lambda i, h, part=part: (i, part * heads + h))
        for part in range(3)
    ]
    return pl.pallas_call(
        functools.partial(attend_kernel, rows, 1.0 / math.sqrt(HEAD_DIM)),
        grid=(seq_count, heads),
        out_shape=jax.ShapeDtypeStruct((qkv.shape[0], heads * HEAD_DIM), BF16),
        in_specs=columns,
        out_specs=columns[0],
        compiler_params=pltpu.CompilerParams(vmem_limit_bytes=48 << 20),
    )(qkv, qkv, qkv)


def attend_back(qkv, back, seq_count, heads):
    seq_len = qkv.shape[0] // seq_count
    rows = min(256, seq_len)
    columns = [
        pl.BlockSpec((seq_len, HEAD_DIM), lambda i, h, part=part: (i, part * heads + h))
        for part in range(3)
    ]
    grads = jax.ShapeDtypeStruct((qkv.shape[0], heads * HEAD_DIM), BF16)
    return pl.pallas_call(
        functools.partial(attend_back_kernel, rows, 1.0 / math.sqrt(HEAD_DIM)),
        grid=(seq_count, heads),
        out_shape=[grads] * 3,
        in_specs=columns + columns[:1],
        out_specs=columns[:1] * 3,
        scratch_shapes=[pltpu.VMEM((seq_len, HEAD_DIM), F32)] * 2,
        compiler_params=pltpu.CompilerParams(vmem_limit_bytes=48 << 20),
    )(qkv, qkv, qkv, back)


def norm_stats(value):
    centre = jnp.mean(value, axis=-1, keepdims=True)
    centred = value - centre
    spread = jnp.mean(centred * centred, axis=-1, keepdims=True)
    inverse = lax.rsqrt(spread + EPS)
    return centred * inverse, inverse


def gelu_parts(value):
    inner = 0.7978845608028654 * (value + 0.044715 * value * value * value)
    return jnp.tanh(inner)


def gelu_tanh(value):
    return 0.5 * value * (1.0 + gelu_parts(value))


def gelu_slope(value):
    tanh = gelu_parts(value)
    rise = 0.7978845608028654 * (1.0 + 3.0 * 0.044715 * value * value)
    return 0.5 * (1.0 + tanh) + 0.5 * value * (1.0 - tanh * tanh) * rise


def local(
    tokens,
    out_cot,
    lengths,
    seq_family,
    family_tokens,
    norm_master,
    attn_bias_master,
    qkv_master,
    proj_master,
    fc_bias_master,
    fc_master,
    down_master,
    norm_moment,
    attn_bias_moment,
    qkv_moment,
    proj_moment,
    fc_bias_moment,
    fc_moment,
    down_moment,
    norm_average,
    attn_bias_average,
    qkv_average,
    proj_average,
    fc_bias_average,
    fc_average,
    down_average,
):
    seq_count = lengths.shape[0]
    row_count = tokens.shape[0]
    seq_len = row_count // seq_count
    family_count = family_tokens.shape[0]
    depth, _, head_width = qkv_master.shape
    local_heads = head_width // HEAD_DIM
    mp_count = lax.axis_size("mp")
    dp_count = lax.axis_size("dp")
    outer = dp_count // 2
    place = lax.axis_index("dp")
    place_out, place_in = place // 2, place % 2
    side = lax.axis_index("mp") % 2
    half = row_count // 2

    def block_at(s, r):
        return ((place_out + (outer - r)) % outer) * 2 + (place_in + s) % 2

    def to_local(value):
        parts = [
            lax.dynamic_slice_in_dim(value, block_at(s, r) * depth, depth, 1)
            for s in range(2)
            for r in range(outer)
        ]
        return jnp.concatenate(parts, axis=1)

    def own_rows(value):
        return lax.dynamic_slice_in_dim(value, side * half, half, 0)

    def other_rows(value):
        return lax.dynamic_slice_in_dim(value, (1 - side) * half, half, 0)

    def halves_swapped(own, other):
        return jnp.where(
            side == 0,
            jnp.concatenate([own, other], axis=0),
            jnp.concatenate([other, own], axis=0),
        )

    columns = norm_master.shape[1]
    low_norm = jnp.pad(norm_master.astype(BF16).T, ((0, 16 - columns), (0, 0)))
    low_qkv = jnp.moveaxis(qkv_master, 1, 0).astype(BF16)
    low_proj = proj_master.astype(BF16)
    low_fc = fc_master.astype(BF16)
    low_down = down_master.astype(BF16)

    family_ids = jnp.arange(family_count, dtype=jnp.int32)
    member = seq_family == family_ids[None, :]
    local_counts = jnp.sum(jnp.where(member, lengths[:, None], 0), axis=0).astype(F32)
    count_tile = jnp.broadcast_to(jnp.pad(local_counts, (0, 128 - family_count))[None], (8, 128))
    w_norm, all_counts, w_qkv, w_proj, w_fc = gather_rows(
        [low_norm, count_tile, low_qkv, low_proj, low_fc], (1, 1, 2, 2, 8), (3, 8, 13), 0
    )
    w_norm = jnp.moveaxis(w_norm.reshape(dp_count, 16, depth), 0, 1).reshape(16, dp_count * depth)
    counts = jnp.sum(all_counts.reshape(dp_count, 8, 128)[:, 0], axis=0)[:family_count]
    low_down, w_fc = lax.optimization_barrier((low_down, w_fc))
    w_down = lax.all_gather(low_down, "dp", axis=0, tiled=True)

    valid_total = jnp.sum(counts)
    share = family_tokens.astype(F32) / jnp.sum(family_tokens).astype(F32)
    family_weight = share * valid_total / jnp.maximum(counts, float(LEN // 2))
    seq_weight = jnp.sum(jnp.where(member, family_weight[None, :], 0.0), axis=1)
    places = jnp.arange(seq_len, dtype=jnp.int32)
    token_weight = jnp.where(places[None, :] < lengths[:, None], seq_weight[:, None], 0.0).reshape(
        row_count
    )

    norm_full = w_norm.astype(F32)
    gain1, shift1, gain2, shift2, bias_p, bias_d = [norm_full[i][None] for i in range(6)]
    bias_row = jnp.concatenate(
        [attn_bias_master[0], jnp.zeros_like(attn_bias_master[0]), attn_bias_master[1]], axis=0
    )
    x_low = tokens
    cot_low = out_cot

    x_hat, _ = norm_stats(x_low.astype(F32))
    ln1_low = (x_hat * gain1 + shift1).astype(BF16)
    qkv = (dot_f32("td,de->te", ln1_low, w_qkv) + bias_row[None]).astype(BF16)
    mixed_low = attend(qkv, seq_count, local_heads)
    mixed_low = halves_swapped(mixed_low[:half], mixed_low[half:])

    def sum_over_cores(product, left):
        other = swap(product(left[half:]).astype(BF16), "mp", 1)
        return (product(left[:half]) + other.astype(F32)).astype(BF16)

    def sum_over_mp(product, left):
        part = sum_over_cores(product, left)
        flip = 2
        while flip < mp_count:
            part = part.astype(F32) + swap(part, "mp", flip).astype(F32)
            flip *= 2
            if flip < mp_count:
                part = part.astype(BF16)
        return part.astype(F32)

    x_own = own_rows(x_low).astype(F32)
    attn_out = sum_over_mp(lambda rows: dot_f32("te,de->td", rows, w_proj), mixed_low)
    residual = x_own + attn_out + bias_p
    hat2, inverse2 = norm_stats(residual)
    ln2_own = (hat2 * gain2 + shift2).astype(BF16)
    ln2_low = jnp.concatenate([ln2_own, swap(ln2_own, "mp", 1)], axis=0)
    pre_act = dot_f32("td,df->tf", ln2_low, w_fc) + fc_bias_master[None]
    hidden_low = gelu_tanh(pre_act).astype(BF16)

    weight_own, weight_other = own_rows(token_weight), other_rows(token_weight)
    upstream = weight_own[:, None] * own_rows(cot_low).astype(F32)
    upstream_other = weight_other[:, None] * other_rows(cot_low).astype(F32)
    upstream_low = jnp.concatenate([upstream, upstream_other], axis=0).astype(BF16)

    def scatter_product(product):
        return lax.psum_scatter(product, "dp", scatter_dimension=0, tiled=True)

    down_product = dot_f32("td,tf->df", upstream_low, hidden_low).astype(BF16)
    down_reduced = scatter_product(down_product)

    back_act = dot_f32("td,df->tf", upstream_low, w_down)
    back_pre = (back_act * gelu_slope(pre_act)).astype(BF16)
    fc_bias_sum = jnp.sum(back_pre, axis=0, dtype=F32)
    fc_product = dot_f32("td,tf->df", ln2_low, back_pre).astype(BF16)

    def norm_back(back, hat, inverse, gain):
        scaled = back * gain
        mean = jnp.mean(scaled, axis=-1, keepdims=True)
        slope = jnp.mean(scaled * hat, axis=-1, keepdims=True)
        return inverse * (scaled - mean - hat * slope)

    back_ln2 = sum_over_mp(lambda rows: dot_f32("tf,df->td", rows, w_fc), back_pre)
    mlp_part = sum_over_cores(lambda rows: dot_f32("tf,df->td", rows, w_down), hidden_low)
    fc_product, mlp_part, back_ln2 = lax.optimization_barrier((fc_product, mlp_part, back_ln2))
    fc_reduced = scatter_product(fc_product)
    gain2_sum = jnp.sum(back_ln2 * hat2, axis=0)
    shift2_sum = jnp.sum(back_ln2, axis=0)
    back_resid = upstream + norm_back(back_ln2, hat2, inverse2, gain2)
    ga_own = back_resid.astype(BF16)
    ga_low = jnp.concatenate([ga_own, swap(ga_own, "mp", 1)], axis=0)
    back_mixed = dot_f32("td,de->te", ga_low, w_proj).astype(BF16)
    back_mixed = halves_swapped(back_mixed[:half], back_mixed[half:])
    back_qkv = jnp.concatenate(attend_back(qkv, back_mixed, seq_count, local_heads), axis=1)
    attn_bias_sum = jnp.sum(back_qkv, axis=0, dtype=F32).reshape(3, head_width)[0::2]
    back_qkv_local = halves_swapped(back_qkv[:half], back_qkv[half:])
    back_part = sum_over_cores(lambda rows: dot_f32("te,de->td", rows, w_qkv), back_qkv_local)
    qkv_part = dot_f32("td,te->de", to_local(ln1_low), back_qkv).astype(BF16)
    proj_part = dot_f32("td,te->de", to_local(ga_low), mixed_low).astype(BF16)
    total_tile = jnp.broadcast_to(valid_total, (8, 128))
    (qkv_raw, proj_raw), square, (back_taken, mlp_taken) = reduce_rows(
        [qkv_part, proj_part], total_tile, [back_part, mlp_part], (4, 1), 1
    )
    back_ln1 = back_part.astype(F32) + back_taken.astype(F32)
    mlp_out = mlp_part.astype(F32) + mlp_taken.astype(F32)
    block_own = (residual + mlp_out + bias_d).astype(BF16)
    hat1, inverse1 = norm_stats(x_own)
    gain1_sum = jnp.sum(back_ln1 * hat1, axis=0)
    shift1_sum = jnp.sum(back_ln1, axis=0)
    whole_own = back_resid + norm_back(back_ln1, hat1, inverse1, gain1)

    norm_part = jnp.stack(
        [
            gain1_sum,
            shift1_sum,
            gain2_sum,
            shift2_sum,
            jnp.sum(back_resid, axis=0),
            jnp.sum(upstream, axis=0),
            jnp.zeros_like(gain1_sum),
            jnp.zeros_like(gain1_sum),
        ],
        axis=0,
    )
    norm_part = jnp.moveaxis(norm_part.reshape(8, dp_count, depth), 1, 0)
    bias_part = jnp.concatenate([attn_bias_sum.reshape(-1), fc_bias_sum]).reshape(-1, 128)
    for reduced in (fc_reduced, down_reduced):
        raw = reduced.astype(F32) / valid_total
        square = square + jnp.sum(raw * raw)
    norm_raw, bias_raw, square, whole_other = finish_sums(
        norm_part, bias_part, square, total_tile, whole_own, 2
    )
    whole = merge_halves(side, whole_own, whole_other)
    block_part = merge_halves(side, block_own, swap(block_own, "mp", 1))
    grad_norm = jnp.sqrt(square[0, 0])
    bias_raw = bias_raw.reshape(-1)
    raw_grads = [
        norm_raw[:columns],
        bias_raw[: 2 * head_width].reshape(2, head_width),
        bias_raw[2 * head_width :].reshape(1, -1),
        qkv_raw,
        proj_raw,
        fc_reduced,
        down_reduced,
    ]
    masters = (
        norm_master,
        attn_bias_master,
        qkv_master,
        proj_master,
        fc_bias_master,
        fc_master,
        down_master,
    )
    moments = (
        norm_moment,
        attn_bias_moment,
        qkv_moment,
        proj_moment,
        fc_bias_moment,
        fc_moment,
        down_moment,
    )
    averages = (
        norm_average,
        attn_bias_average,
        qkv_average,
        proj_average,
        fc_bias_average,
        fc_average,
        down_average,
    )
    order = (0, 1, 4, 2, 3, 5, 6)

    def arranged(values):
        values = [values[i] for i in order]
        values[0] = values[0].T
        values[2] = values[2].reshape(1, -1)
        values[3] = jnp.moveaxis(values[3], 1, 0)
        return values

    def returned(values):
        values = list(values)
        values[0] = values[0].T
        values[2] = values[2].reshape(-1)
        values[3] = jnp.moveaxis(values[3], 0, 1)
        return [values[order.index(i)] for i in range(7)]

    grads_out, momenta_out, averaged_out, updated_out, copies_out = [
        returned(values)
        for values in step_all(
            square, total_tile, raw_grads, arranged(masters), arranged(moments), arranged(averages), 3
        )
    ]
    return (
        block_part,
        whole,
        grads_out[0],
        grads_out[1],
        grads_out[2],
        grads_out[3],
        grads_out[4],
        grads_out[5],
        grads_out[6],
        momenta_out[0],
        momenta_out[1],
        momenta_out[2],
        momenta_out[3],
        momenta_out[4],
        momenta_out[5],
        momenta_out[6],
        averaged_out[0],
        averaged_out[1],
        averaged_out[2],
        averaged_out[3],
        averaged_out[4],
        averaged_out[5],
        averaged_out[6],
        updated_out[0],
        updated_out[1],
        updated_out[2],
        updated_out[3],
        updated_out[4],
        updated_out[5],
        updated_out[6],
        copies_out[0],
        copies_out[1],
        copies_out[2],
        copies_out[3],
        copies_out[4],
        copies_out[5],
        copies_out[6],
        grad_norm,
    )


def solution(mesh):
    placed = (
        P("dp", None),
        P("dp", None),
        P("dp"),
        P("dp", None),
        P(),
        P("dp", None),
        P(None, "mp"),
        P("dp", None, "mp"),
        P("dp", "mp"),
        P("mp"),
        P("dp", "mp"),
        P("dp", "mp"),
        P("dp", None),
        P(None, "mp"),
        P("dp", None, "mp"),
        P("dp", "mp"),
        P("mp"),
        P("dp", "mp"),
        P("dp", "mp"),
        P("dp", None),
        P(None, "mp"),
        P("dp", None, "mp"),
        P("dp", "mp"),
        P("mp"),
        P("dp", "mp"),
        P("dp", "mp"),
    )
    return jax.shard_map(
        local,
        mesh=mesh,
        in_specs=placed,
        out_specs=(
            P("dp", None),
            P("dp", None),
            P("dp", None),
            P(None, "mp"),
            P("dp", None, "mp"),
            P("dp", "mp"),
            P("mp"),
            P("dp", "mp"),
            P("dp", "mp"),
            P("dp", None),
            P(None, "mp"),
            P("dp", None, "mp"),
            P("dp", "mp"),
            P("mp"),
            P("dp", "mp"),
            P("dp", "mp"),
            P("dp", None),
            P(None, "mp"),
            P("dp", None, "mp"),
            P("dp", "mp"),
            P("mp"),
            P("dp", "mp"),
            P("dp", "mp"),
            P("dp", None),
            P(None, "mp"),
            P("dp", None, "mp"),
            P("dp", "mp"),
            P("mp"),
            P("dp", "mp"),
            P("dp", "mp"),
            P("dp", None),
            P(None, "mp"),
            P("dp", None, "mp"),
            P("dp", "mp"),
            P("mp"),
            P("dp", "mp"),
            P("dp", "mp"),
            P(),
        ),
        check_vma=False,
    )
```

```python
import functools
import math

import jax
import jax.numpy as jnp
from jax import lax
from jax.experimental import pallas as pl
from jax.experimental.pallas import tpu as pltpu
from jax.sharding import PartitionSpec as P

HEAD_DIM = 128
LEN = 1024


EPS = 1e-05
MOMENTUM = 0.9
RATE = 192.0
KEEP = 0.9
NEG = -1e30
BF16 = jnp.bfloat16
F32 = jnp.float32
MESH = pl.DeviceIdType.MESH


def dot_f32(eq, left, right):
    return jnp.einsum(eq, left, right, preferred_element_type=F32)


def swap(value, axis, flip):
    size = lax.axis_size(axis)
    return lax.ppermute(value, axis, [(i, i ^ flip) for i in range(size)])


def gather_kernel(outer, pieces, count, *refs):
    shards, wholes = refs[:count], refs[count : 2 * count]
    send, recv, local = refs[2 * count :]
    me = lax.axis_index("dp")
    out, side = me // 2, me % 2
    pair = out * 2 + 1 - side
    hops = outer - 1
    total = len(pieces)
    line = ((0, 1), (1, -1))

    def has(way, steps):
        return out >= steps if way > 0 else out + steps < outer

    def follows(way):
        return out + 1 < outer if way > 0 else out >= 1

    barrier = pltpu.get_barrier_semaphore()
    for peer in [lax.rem(out + r, outer) * 2 + side for r in range(1, outer)] + [pair]:
        pl.semaphore_signal(barrier, inc=1, device_id={"dp": peer}, device_id_type=MESH)
    pl.semaphore_wait(barrier, outer)

    def slot(p, device):
        a, plane, start, rows, _ = pieces[p]
        depth = shards[a].shape[-2]
        where = pl.ds(device * depth + start, rows)
        if plane is None:
            return wholes[a].at[where]
        width = shards[a].shape[-1]
        return wholes[a].at[where, pl.ds(plane * width, width)]

    def own(p):
        a, plane, start, rows, _ = pieces[p]
        where = pl.ds(start, rows)
        return shards[a].at[where] if plane is None else shards[a].at[plane, where]

    def remote(p, lane, source, target, peer):
        return pltpu.make_async_remote_copy(
            src_ref=source,
            dst_ref=target,
            send_sem=send.at[p, lane],
            recv_sem=recv.at[p, lane],
            device_id={"dp": peer},
            device_id_type=MESH,
        )

    def pass_on(p, other, index, way, steps):
        origin = (out - way * (steps - 1)) * 2 + (1 - side if other else side)
        here = slot(p, origin)
        source = own(p) if steps == 1 and not other else here
        lane = (2 * int(other) + index) * hops + steps - 1
        return remote(p, lane, source, here, (out + way) * 2 + side)

    def arrival(p, other, index, way, steps):
        origin = (out - way * steps) * 2 + (1 - side if other else side)
        lane = (2 * int(other) + index) * hops + steps - 1
        return remote(p, lane, slot(p, origin), slot(p, origin), pair)

    def to_pair(p, index, way, steps):
        if steps == 0:
            return remote(p, 4 * hops, own(p), slot(p, me), pair)
        here = slot(p, (out - way * steps) * 2 + side)
        return remote(p, (2 + index) * hops + steps - 1, here, here, pair)

    def begin(p):
        to_pair(p, 0, 1, 0).start()
        pltpu.make_async_copy(own(p), slot(p, me), local.at[p]).start()
        for index, way in line:

            @pl.when(follows(way))
            def _():
                pass_on(p, False, index, way, 1).start()

    def proceed(p, other, steps):
        early = pieces[p][4]
        for index, way in line:

            @pl.when(has(way, steps))
            def _():
                arrival(p, other, index, way, steps).wait_recv()
                if not early:
                    to_pair(p, index, way, steps).start()

            if steps < hops:

                @pl.when(jnp.logical_and(has(way, steps), follows(way)))
                def _():
                    pass_on(p, other, index, way, steps + 1).start()

    def cross(p):
        to_pair(p, 0, 1, 0).wait_recv()
        for index, way in line:

            @pl.when(follows(way))
            def _():
                pass_on(p, True, index, way, 1).start()

    lead = 4
    for p in range(min(lead, total)):
        begin(p)
    for wave in range(total + outer):
        if wave + lead < total:
            begin(wave + lead)
        if wave < total and pieces[wave][4]:
            cross(wave)
        for steps in range(1, outer):
            p = wave - steps + 1
            if 0 <= p < total:
                proceed(p, False, steps)
            p -= 1
            if 0 <= p < total and pieces[p][4]:
                proceed(p, True, steps)
    for p in range(total):
        early = pieces[p][4]
        to_pair(p, 0, 1, 0).wait_send()
        if not early:
            to_pair(p, 0, 1, 0).wait_recv()
        pltpu.make_async_copy(own(p), slot(p, me), local.at[p]).wait()
        for index, way in line:
            for other in (False, True) if early else (False,):
                for steps in range(1, outer):

                    @pl.when(jnp.logical_and(has(way, steps - 1), follows(way)))
                    def _():
                        pass_on(p, other, index, way, steps).wait_send()

            if not early:
                for steps in range(1, outer):

                    @pl.when(has(way, steps))
                    def _():
                        to_pair(p, index, way, steps).wait_send()
                        remote(
                            p,
                            (2 + index) * hops + steps - 1,
                            slot(p, me),
                            slot(p, (out - way * steps) * 2 + 1 - side),
                            pair,
                        ).wait_recv()


def gather_rows(shards, cuts, early, collective_id):
    size = lax.axis_size("dp")
    outer = size // 2
    count = len(shards)
    pieces, shapes = [], []
    for a, shard in enumerate(shards):
        depth, width = shard.shape[-2:]
        planes = [None] if shard.ndim == 2 else list(range(shard.shape[0]))
        rows = depth // cuts[a]
        for plane in planes:
            for i in range(cuts[a]):
                pieces.append((a, plane, i * rows, rows, len(pieces) in early))
        shapes.append(jax.ShapeDtypeStruct((size * depth, width * len(planes)), shard.dtype))
    anywhere = pl.BlockSpec(memory_space=pl.ANY)
    lanes = pltpu.SemaphoreType.DMA((len(pieces), 4 * outer - 3))
    return pl.pallas_call(
        functools.partial(gather_kernel, outer, pieces, count),
        out_shape=shapes,
        in_specs=[anywhere] * count,
        out_specs=[anywhere] * count,
        scratch_shapes=[lanes, lanes, pltpu.SemaphoreType.DMA((len(pieces),))],
        compiler_params=pltpu.CompilerParams(collective_id=collective_id, has_side_effects=True),
    )(*shards)


def remote_copy(source, target, send_sem, recv_sem, device):
    return pltpu.make_async_remote_copy(
        src_ref=source,
        dst_ref=target,
        send_sem=send_sem,
        recv_sem=recv_sem,
        device_id=device,
        device_id_type=MESH,
    )


def last_kernel(dp_count, mp_count, depth, pieces, count, tile_rows, *refs):
    refs = list(refs)

    def take(number):
        return [refs.pop(0) for _ in range(number)]

    grads = take(count)
    crossed = take(2)
    x_hbm, back_hbm, resid_hbm, total_ref, gain_ref, shift_ref, norm_ref, bias_ref = take(8)
    raws = take(count)
    square_ref, norm_out, bias_out, whole_out, block_out = take(5)
    bits = dp_count.bit_length() - 1
    own = take(count)
    got = [take(count) for _ in range(bits)]
    parts, taken = take(2), take(2)
    x_ref, back_ref, resid_ref, block_ref, sums, norm_own, norm_in, bias_in = take(8)
    half_send, half_recv, local, loading = take(4)
    cross_send, cross_recv, norm_send, norm_recv, bias_send, bias_recv = take(6)
    core_send, core_recv, placing = take(3)

    me, across = lax.axis_index("dp"), lax.axis_index("mp")
    mine = [me // (1 << bit) % 2 for bit in range(bits)]
    falling = list(reversed(range(bits)))
    core = across % 2
    near = across + 1 - 2 * core
    other = {"mp": lax.rem(across + 2, 4)}
    half = x_ref.shape[0]

    def spot(kd, flip):
        return {"dp": lax.rem(me + kd, dp_count), "mp": near if flip else across}

    hops = [(kd, flip) for kd in range(dp_count) for flip in range(2)][1:]
    barrier = pltpu.get_barrier_semaphore()
    for kd, flip in hops:
        pl.semaphore_signal(barrier, inc=1, device_id=spot(kd, flip), device_id_type=MESH)
    pl.semaphore_signal(barrier, inc=1, device_id=other, device_id_type=MESH)
    pl.semaphore_wait(barrier, len(hops) + 1)

    crosses = [
        remote_copy(crossed[i], taken[i], cross_send.at[i], cross_recv.at[i], other)
        for i in range(2)
    ]
    crosses[0].start()

    everything = slice(None)

    def first_index(p, value):
        return tuple(value if bit == pieces[p][3][0] else everything for bit in falling)

    def index(p, phase, value):
        order = pieces[p][3]
        place = []
        for bit in falling:
            if bit in order[1:phase]:
                place.append(mine[bit])
            elif phase and bit == order[phase]:
                place.append(value)
            elif bit != order[0]:
                place.append(everything)
        return tuple(place)

    def trade(p, phase):
        a, start, rows, order = pieces[p]
        bit, rows = order[phase], (pl.ds(start, rows),)
        if phase:
            source = own[a].at[index(p, phase, 1 - mine[bit]) + rows]
        else:
            source = grads[a].at[first_index(p, 1 - mine[bit]) + rows]
        return remote_copy(
            source,
            got[phase][a].at[(everything,) * (bits - 1 - phase) + rows],
            half_send.at[p, phase],
            half_recv.at[p, phase],
            {"dp": me + (1 - 2 * mine[bit]) * (1 << bit)},
        )

    def load(p):
        a, start, rows, order = pieces[p]
        rows = (pl.ds(start, rows),)
        return pltpu.make_async_copy(
            grads[a].at[first_index(p, mine[order[0]]) + rows],
            own[a].at[(everything,) * (bits - 1) + rows],
            local.at[p],
        )

    lead, skew = 6, 2
    for p in range(min(lead, len(pieces))):
        trade(p, 0).start()
    for p in range(len(pieces)):
        load(p).start()
    later = [
        pltpu.make_async_copy(source, target, loading.at[i])
        for i, (source, target) in enumerate(
            [
                (crossed[0], parts[0]),
                (crossed[1], parts[1]),
                (x_hbm, x_ref),
                (back_hbm, back_ref),
                (resid_hbm, resid_ref),
            ]
        )
    ]
    for copy in later:
        copy.start()
    norm_own[...] = norm_ref[...]
    bias_in[me] = bias_ref[...]
    bias_copies = [
        remote_copy(bias_ref, bias_in.at[me], bias_send.at[kd], bias_recv.at[kd], spot(kd, 0))
        for kd in range(1, dp_count)
    ]
    for copy in bias_copies:
        copy.start()
    total = total_ref[0:1, 0:1]
    squares = []

    def finish(p, phase):
        a, start, rows, order = pieces[p]
        rows = (pl.ds(start, rows),)
        if phase == 0:
            load(p).wait()
        trade(p, phase).wait_recv()
        if phase == 0 and p + lead < len(pieces):
            trade(p + lead, 0).start()
        kept = index(p, phase, mine[order[phase]]) + rows
        both = own[a][kept].astype(F32)
        both = both + got[phase][a][(everything,) * (bits - 1 - phase) + rows].astype(F32)
        if phase < bits - 1:
            own[a][kept] = both.astype(BF16)
            trade(p, phase + 1).start()
        else:
            raw = both / total
            raws[a][rows] = raw
            squares.append(jnp.sum(raw * raw, keepdims=True))

    waves = len(pieces) + skew * (bits - 1)

    def advance(first, last):
        for wave in range(first, last):
            for phase in range(bits):
                if 0 <= wave - skew * phase < len(pieces):
                    finish(wave - skew * phase, phase)

    middle, later_on = 2 * waves // 5, 4 * waves // 5
    advance(0, middle)

    for copy in later:
        copy.wait()
    crosses[0].wait_recv()
    crosses[1].start()
    sums[...] = jnp.zeros_like(sums)
    gain = gain_ref[0:1]

    @pl.loop(0, half // tile_rows)
    def _(i):
        where = pl.ds(pl.multiple_of(i * tile_rows, tile_rows), tile_rows)
        hat, inverse = norm_stats(x_ref[where].astype(F32))
        back = parts[0][where].astype(F32) + taken[0][where].astype(F32)
        product = back * hat
        sums[0] += jnp.sum(product.reshape(tile_rows // 8, 8, -1), axis=0)
        sums[1] += jnp.sum(back.reshape(tile_rows // 8, 8, -1), axis=0)
        back_ref[where] = back_ref[where] + norm_back(back, hat, inverse, gain)

    whole_place = pl.ds(pl.multiple_of(core * half, half), half)
    whole_copy = remote_copy(
        back_ref, whole_out.at[whole_place], core_send.at[0], core_recv.at[0], spot(0, 1)
    )
    whole_copy.start()
    whole_local = pltpu.make_async_copy(back_ref, whole_out.at[whole_place], placing.at[0])
    whole_local.start()
    for k in range(2):
        row = jnp.sum(sums[k], axis=0, keepdims=True)
        for d in range(dp_count):
            norm_own[d, k : k + 1] = row[:, d * depth : (d + 1) * depth]
    norm_copies = [
        remote_copy(
            norm_own.at[lax.rem(me + kd, dp_count)],
            norm_in.at[me * 2 + core],
            norm_send.at[kd, flip],
            norm_recv.at[kd, flip],
            spot(kd, flip),
        )
        for kd, flip in hops
    ]
    for copy in norm_copies:
        copy.start()
    norm_in[me * 2 + core] = norm_own[me]

    advance(middle, later_on)

    crosses[1].wait_recv()
    shift = shift_ref[0:1]

    @pl.loop(0, half // tile_rows)
    def _(i):
        where = pl.ds(pl.multiple_of(i * tile_rows, tile_rows), tile_rows)
        mlp = parts[1][where].astype(F32) + taken[1][where].astype(F32)
        block_ref[where] = (resid_ref[where] + mlp + shift).astype(BF16)

    block_copy = remote_copy(
        block_ref, block_out.at[whole_place], core_send.at[1], core_recv.at[1], spot(0, 1)
    )
    block_copy.start()
    block_local = pltpu.make_async_copy(block_ref, block_out.at[whole_place], placing.at[1])
    block_local.start()
    advance(later_on, waves)

    for copy in norm_copies + bias_copies:
        copy.wait_recv()
    norm = norm_in[0]
    for i in range(1, 2 * dp_count):
        norm = norm + norm_in[i]
    bias = bias_in[0]
    for i in range(1, dp_count):
        bias = bias + bias_in[i]
    norm = norm / total
    bias = bias / total
    norm_out[...] = norm
    bias_out[...] = bias
    square = jnp.sum(norm * norm, keepdims=True) / float(mp_count)
    square = square + jnp.sum(bias * bias, keepdims=True) / float(dp_count)

    for part in squares:
        square = square + part
    square_ref[...] = jnp.broadcast_to(square, square_ref.shape)
    for p in range(len(pieces)):
        for phase in range(bits):
            trade(p, phase).wait_send()
    for copy in crosses + norm_copies + bias_copies:
        copy.wait_send()
    whole_copy.wait()
    whole_local.wait()
    block_copy.wait()
    block_local.wait()


def last_sums(grads, crossed, x_own, back, residual, total, gain, shift, norm_part, bias_part):
    dp_count, mp_count = lax.axis_size("dp"), lax.axis_size("mp")
    bits = dp_count.bit_length() - 1
    count, depth = len(grads), grads[0].shape[0] // dp_count
    half, width = x_own.shape
    straight = list(range(bits))
    turned = [1, 0] + straight[2:]
    pieces = []
    for a, grad in enumerate(grads):
        rows = max(16, depth * 256 // grad.shape[1] // 4)
        rows = min(rows // 16 * 16, depth)
        number = depth // rows
        for i in range(number):
            order = turned if a == 0 and i % 2 == 0 else straight
            pieces.append(((2 * i + 1) / number, (a, i * rows, rows, order)))
    pieces = [piece for _, piece in sorted(pieces, key=lambda piece: piece[0])]
    anywhere = pl.BlockSpec(memory_space=pl.ANY)
    inside = pl.BlockSpec(memory_space=pltpu.VMEM)

    def blocks(number):
        return [pltpu.VMEM((2,) * number + (depth, grad.shape[1]), BF16) for grad in grads]

    slim, wide = pltpu.VMEM((half, width), BF16), pltpu.VMEM((half, width), F32)
    dma = pltpu.SemaphoreType.DMA
    results = pl.pallas_call(
        functools.partial(last_kernel, dp_count, mp_count, depth, pieces, count, min(64, half)),
        out_shape=[jax.ShapeDtypeStruct((depth, grad.shape[1]), F32) for grad in grads]
        + [
            jax.ShapeDtypeStruct((8, 128), F32),
            jax.ShapeDtypeStruct(norm_part.shape[1:], F32),
            jax.ShapeDtypeStruct(bias_part.shape, F32),
            jax.ShapeDtypeStruct((2 * half, width), F32),
            jax.ShapeDtypeStruct((2 * half, width), BF16),
        ],
        in_specs=[anywhere] * (count + 5) + [inside] * 5,
        out_specs=[inside] * (count + 3) + [anywhere] * 2,
        scratch_shapes=blocks(bits - 1)
        + sum([blocks(bits - 1 - phase) for phase in range(bits)], [])
        + [slim] * 4
        + [slim, wide, wide, slim]
        + [
            pltpu.VMEM((2, 8, width), F32),
            pltpu.VMEM(norm_part.shape, F32),
            pltpu.VMEM((2 * dp_count, *norm_part.shape[1:]), F32),
            pltpu.VMEM((dp_count, *bias_part.shape), F32),
        ]
        + [dma((len(pieces), bits))] * 2
        + [dma((len(pieces),)), dma((5,))]
        + [dma((2,))] * 2
        + [dma((dp_count, 2))] * 2
        + [dma((dp_count,))] * 2
        + [dma((2,))] * 3,
        compiler_params=pltpu.CompilerParams(
            collective_id=1, has_side_effects=True, vmem_limit_bytes=58 << 20
        ),
    )(
        *[grad.reshape((2,) * bits + (depth, -1)) for grad in grads],
        *crossed,
        x_own,
        back,
        residual,
        total,
        gain,
        shift,
        norm_part,
        bias_part,
    )
    return results[:count], *results[count:]


def everyone(dp_count, mp_count):
    return [(kd, km) for kd in range(dp_count) for km in range(mp_count)][1:]


def square_kernel(dp_count, mp_count, count, tile_ref, total_ref, *refs):
    summed, (out_ref, tiles, own_ref, send, recv) = refs[:count], refs[count:]
    me, across = lax.axis_index("dp"), lax.axis_index("mp")
    hops = everyone(dp_count, mp_count)

    def spot(kd, km):
        return {"dp": lax.rem(me + kd, dp_count), "mp": lax.rem(across + km, mp_count)}

    barrier = pltpu.get_barrier_semaphore()
    for kd, km in hops:
        pl.semaphore_signal(barrier, inc=1, device_id=spot(kd, km), device_id_type=MESH)
    total = total_ref[0:1, 0:1]
    square = tile_ref[...]
    for ref in summed:
        raw = ref[...].astype(F32) / total
        square = square + jnp.sum(raw * raw)
    own_ref[...] = square
    pl.semaphore_wait(barrier, len(hops))
    slot = me * mp_count + across
    copies = [
        remote_copy(own_ref, tiles.at[slot], send.at[i], recv.at[i], spot(kd, km))
        for i, (kd, km) in enumerate(hops)
    ]
    for copy in copies:
        copy.start()
    tiles[slot] = own_ref[...]
    for copy in copies:
        copy.wait_recv()
    square = tiles[0]
    for i in range(1, dp_count * mp_count):
        square = square + tiles[i]
    out_ref[...] = square
    for copy in copies:
        copy.wait_send()


def sum_everywhere(tile, total, summed, collective_id):
    dp_count, mp_count = lax.axis_size("dp"), lax.axis_size("mp")
    inside = pl.BlockSpec(memory_space=pltpu.VMEM)
    hops = pltpu.SemaphoreType.DMA((dp_count * mp_count - 1,))
    return pl.pallas_call(
        functools.partial(square_kernel, dp_count, mp_count, len(summed)),
        out_shape=jax.ShapeDtypeStruct(tile.shape, F32),
        in_specs=[inside] * (2 + len(summed)),
        out_specs=inside,
        scratch_shapes=[
            pltpu.VMEM((dp_count * mp_count, *tile.shape), F32),
            pltpu.VMEM(tile.shape, F32),
            hops,
            hops,
        ],
        compiler_params=pltpu.CompilerParams(
            collective_id=collective_id, has_side_effects=True, vmem_limit_bytes=16 << 20
        ),
    )(tile, total, *summed)


def step_kernel(splits, divided, whole_count, square_ref, total_ref, *refs):
    count = len(splits)
    refs = list(refs)
    raws = [[refs.pop(0) for _ in range(number)] for number in splits]
    masters, moments, averages = [refs[i * count : (i + 1) * count] for i in range(3)]
    outs = [refs[(3 + i) * count : (4 + i) * count] for i in range(5)]
    clip = jnp.minimum(1.0, 1.0 / (jnp.sqrt(square_ref[0:1, 0:1]) + 1e-06))
    total = total_ref[0:1, 0:1]

    def update(raw, master, moment, average):
        clipped = raw * clip
        momentum = MOMENTUM * moment + clipped
        updated = master - RATE * (clipped + MOMENTUM * momentum)
        averaged = KEEP * average + (1.0 - KEEP) * updated
        return clipped, momentum, averaged, updated, updated.astype(BF16)

    def apply(a):
        if len(masters[a].shape) == 2:
            raw = [part[...].astype(F32) for part in raws[a]]
            raw = raw[0] if len(raw) == 1 else jnp.concatenate(raw, axis=1)
            if a >= divided:
                raw = raw / total
            results = update(raw, masters[a][...], moments[a][...], averages[a][...])
            for out, result in zip(outs, results):
                out[a][...] = result
        else:
            width = masters[a].shape[2]
            for c in range(masters[a].shape[0]):
                results = update(
                    raws[a][0][:, c * width : (c + 1) * width],
                    masters[a][c],
                    moments[a][c],
                    averages[a][c],
                )
                for out, result in zip(outs, results):
                    out[a][c] = result

    for a in range(whole_count, count):
        apply(a)

    @pl.when(pl.program_id(0) == 0)
    def _():
        for a in range(whole_count):
            apply(a)


def step_all(square, total, raws, masters, moments, averages, whole_count, divided):
    raws = [raw if isinstance(raw, tuple) else (raw,) for raw in raws]
    depth = raws[-1][0].shape[0]
    rows = min(32, depth)

    def spec(value, a):
        shape = value.shape
        if a < whole_count:
            return pl.BlockSpec(shape, lambda i, n=len(shape): (0,) * n)
        if len(shape) == 3:
            return pl.BlockSpec((shape[0], rows, shape[2]), lambda i: (0, i, 0))
        return pl.BlockSpec((rows, shape[1]), lambda i: (i, 0))

    def specs(values):
        return [spec(value, a) for a, value in enumerate(values)]

    tile = pl.BlockSpec((8, 128), lambda i: (0, 0))
    wide = [jax.ShapeDtypeStruct(master.shape, F32) for master in masters]
    slim = [jax.ShapeDtypeStruct(master.shape, BF16) for master in masters]
    results = pl.pallas_call(
        functools.partial(step_kernel, [len(raw) for raw in raws], divided, whole_count),
        grid=(depth // rows,),
        out_shape=wide * 4 + slim,
        in_specs=[tile, tile]
        + [spec(part, a) for a, raw in enumerate(raws) for part in raw]
        + specs(masters) * 3,
        out_specs=specs(masters) * 5,
        compiler_params=pltpu.CompilerParams(vmem_limit_bytes=56 << 20),
    )(square, total, *sum(raws, ()), *masters, *moments, *averages)
    count = len(masters)
    return [results[i * count : (i + 1) * count] for i in range(5)]


def score_block(query_ref, key_ref, first, rows, scale):
    width = first + rows
    scores = scale * lax.dot_general(
        query_ref[first:width], key_ref[:width], (((1,), (1,)), ((), ())), preferred_element_type=F32
    )
    row = first + lax.broadcasted_iota(jnp.int32, (rows, width), 0)
    column = lax.broadcasted_iota(jnp.int32, (rows, width), 1)
    scores = jnp.where(column <= row, scores, NEG)
    raised = jnp.exp(scores - jnp.max(scores, axis=-1, keepdims=True))
    return raised / jnp.sum(raised, axis=-1, keepdims=True)


def attend_kernel(rows, scale, query_ref, key_ref, value_ref, out_ref):
    for first in range(0, query_ref.shape[0], rows):
        prob = score_block(query_ref, key_ref, first, rows, scale)
        out_ref[first : first + rows] = jnp.dot(
            prob.astype(BF16), value_ref[: first + rows], preferred_element_type=F32
        ).astype(BF16)


def attend_back_kernel(
    rows, scale, query_ref, key_ref, value_ref, back_ref, gq_ref, gk_ref, gv_ref, key_sum, value_sum
):
    key_sum[...] = jnp.zeros_like(key_sum)
    value_sum[...] = jnp.zeros_like(value_sum)
    over_rows = (((0,), (0,)), ((), ()))
    for first in range(0, query_ref.shape[0], rows):
        width = first + rows
        prob = score_block(query_ref, key_ref, first, rows, scale)
        back = back_ref[first:width]
        back_prob = lax.dot_general(
            back, value_ref[:width], (((1,), (1,)), ((), ())), preferred_element_type=F32
        )
        value_sum[:width] += lax.dot_general(
            prob.astype(BF16), back, over_rows, preferred_element_type=F32
        )
        slope = jnp.sum(prob * back_prob, axis=-1, keepdims=True)
        back_score = (prob * (back_prob - slope)).astype(BF16)
        gq_ref[first:width] = (
            scale * jnp.dot(back_score, key_ref[:width], preferred_element_type=F32)
        ).astype(BF16)
        key_sum[:width] += lax.dot_general(
            back_score, query_ref[first:width], over_rows, preferred_element_type=F32
        )
    gk_ref[...] = (scale * key_sum[...]).astype(BF16)
    gv_ref[...] = value_sum[...].astype(BF16)


def attend(qkv, seq_count, heads):
    seq_len = qkv.shape[0] // seq_count
    rows = min(256, seq_len)
    columns = [
        pl.BlockSpec((seq_len, HEAD_DIM), lambda i, h, part=part: (i, part * heads + h))
        for part in range(3)
    ]
    return pl.pallas_call(
        functools.partial(attend_kernel, rows, 1.0 / math.sqrt(HEAD_DIM)),
        grid=(seq_count, heads),
        out_shape=jax.ShapeDtypeStruct((qkv.shape[0], heads * HEAD_DIM), BF16),
        in_specs=columns,
        out_specs=columns[0],
        compiler_params=pltpu.CompilerParams(vmem_limit_bytes=48 << 20),
    )(qkv, qkv, qkv)


def attend_back(qkv, back, seq_count, heads):
    seq_len = qkv.shape[0] // seq_count
    rows = min(256, seq_len)
    columns = [
        pl.BlockSpec((seq_len, HEAD_DIM), lambda i, h, part=part: (i, part * heads + h))
        for part in range(3)
    ]
    grads = jax.ShapeDtypeStruct((qkv.shape[0], heads * HEAD_DIM), BF16)
    return pl.pallas_call(
        functools.partial(attend_back_kernel, rows, 1.0 / math.sqrt(HEAD_DIM)),
        grid=(seq_count, heads),
        out_shape=[grads] * 3,
        in_specs=columns + columns[:1],
        out_specs=columns[:1] * 3,
        scratch_shapes=[pltpu.VMEM((seq_len, HEAD_DIM), F32)] * 2,
        compiler_params=pltpu.CompilerParams(vmem_limit_bytes=48 << 20),
    )(qkv, qkv, qkv, back)


def norm_stats(value):
    centre = jnp.mean(value, axis=-1, keepdims=True)
    centred = value - centre
    spread = jnp.mean(centred * centred, axis=-1, keepdims=True)
    inverse = lax.rsqrt(spread + EPS)
    return centred * inverse, inverse


def norm_back(back, hat, inverse, gain):
    scaled = back * gain
    mean = jnp.mean(scaled, axis=-1, keepdims=True)
    slope = jnp.mean(scaled * hat, axis=-1, keepdims=True)
    return inverse * (scaled - mean - hat * slope)


def gelu_parts(value):
    inner = 0.7978845608028654 * (value + 0.044715 * value * value * value)
    return jnp.tanh(inner)


def gelu_tanh(value):
    return 0.5 * value * (1.0 + gelu_parts(value))


def gelu_slope(value):
    tanh = gelu_parts(value)
    rise = 0.7978845608028654 * (1.0 + 3.0 * 0.044715 * value * value)
    return 0.5 * (1.0 + tanh) + 0.5 * value * (1.0 - tanh * tanh) * rise


def local(
    tokens,
    out_cot,
    lengths,
    seq_family,
    family_tokens,
    norm_master,
    attn_bias_master,
    qkv_master,
    proj_master,
    fc_bias_master,
    fc_master,
    down_master,
    norm_moment,
    attn_bias_moment,
    qkv_moment,
    proj_moment,
    fc_bias_moment,
    fc_moment,
    down_moment,
    norm_average,
    attn_bias_average,
    qkv_average,
    proj_average,
    fc_bias_average,
    fc_average,
    down_average,
):
    seq_count = lengths.shape[0]
    row_count = tokens.shape[0]
    seq_len = row_count // seq_count
    family_count = family_tokens.shape[0]
    depth, _, head_width = qkv_master.shape
    local_heads = head_width // HEAD_DIM
    mp_count = lax.axis_size("mp")
    dp_count = lax.axis_size("dp")
    outer = dp_count // 2
    place = lax.axis_index("dp")
    place_out, place_in = place // 2, place % 2
    side = lax.axis_index("mp") % 2
    half = row_count // 2

    def own_rows(value):
        return lax.dynamic_slice_in_dim(value, side * half, half, 0)

    def other_rows(value):
        return lax.dynamic_slice_in_dim(value, (1 - side) * half, half, 0)

    def halves_swapped(own, other):
        return jnp.where(
            side == 0,
            jnp.concatenate([own, other], axis=0),
            jnp.concatenate([other, own], axis=0),
        )

    columns = norm_master.shape[1]
    low_norm = jnp.pad(norm_master.astype(BF16).T, ((0, 16 - columns), (0, 0)))
    low_qkv = jnp.moveaxis(qkv_master, 1, 0).astype(BF16)
    low_proj = proj_master.astype(BF16)
    low_fc = fc_master.astype(BF16)
    low_down = down_master.astype(BF16)

    family_ids = jnp.arange(family_count, dtype=jnp.int32)
    member = seq_family == family_ids[None, :]
    local_counts = jnp.sum(jnp.where(member, lengths[:, None], 0), axis=0).astype(F32)
    count_tile = jnp.broadcast_to(jnp.pad(local_counts, (0, 128 - family_count))[None], (8, 128))
    w_norm, all_counts, w_qkv, w_proj, w_fc = gather_rows(
        [low_norm, count_tile, low_qkv, low_proj, low_fc], (1, 1, 2, 2, 8), (3, 8, 13), 0
    )
    w_norm = jnp.moveaxis(w_norm.reshape(dp_count, 16, depth), 0, 1).reshape(16, dp_count * depth)
    counts = jnp.sum(all_counts.reshape(dp_count, 8, 128)[:, 0], axis=0)[:family_count]
    low_down, w_fc = lax.optimization_barrier((low_down, w_fc))
    w_down = lax.all_gather(low_down, "dp", axis=0, tiled=True)

    valid_total = jnp.sum(counts)
    share = family_tokens.astype(F32) / jnp.sum(family_tokens).astype(F32)
    family_weight = share * valid_total / jnp.maximum(counts, float(LEN // 2))
    seq_weight = jnp.sum(jnp.where(member, family_weight[None, :], 0.0), axis=1)
    places = jnp.arange(seq_len, dtype=jnp.int32)
    token_weight = jnp.where(places[None, :] < lengths[:, None], seq_weight[:, None], 0.0).reshape(
        row_count
    )

    norm_full = w_norm.astype(F32)
    gain1, shift1, gain2, shift2, bias_p, bias_d = [norm_full[i][None] for i in range(6)]
    bias_row = jnp.concatenate(
        [attn_bias_master[0], jnp.zeros_like(attn_bias_master[0]), attn_bias_master[1]], axis=0
    )
    x_low = tokens
    cot_low = out_cot

    x_hat, _ = norm_stats(x_low.astype(F32))
    ln1_low = (x_hat * gain1 + shift1).astype(BF16)
    qkv = (dot_f32("td,de->te", ln1_low, w_qkv) + bias_row[None]).astype(BF16)
    mixed_low = attend(qkv, seq_count, local_heads)
    mixed_low = halves_swapped(mixed_low[:half], mixed_low[half:])

    def sum_over_cores(product, left):
        other = swap(product(left[half:]).astype(BF16), "mp", 1)
        return (product(left[:half]) + other.astype(F32)).astype(BF16)

    def sum_over_mp(product, left):
        return sum_across(sum_over_cores(product, left))

    def sum_across(part):
        flip = 2
        while flip < mp_count:
            part = part.astype(F32) + swap(part, "mp", flip).astype(F32)
            flip *= 2
            if flip < mp_count:
                part = part.astype(BF16)
        return part.astype(F32)

    x_own = own_rows(x_low)
    attn_out = sum_over_mp(lambda rows: dot_f32("te,de->td", rows, w_proj), mixed_low)
    weight_own, weight_other = own_rows(token_weight), other_rows(token_weight)
    upstream = weight_own[:, None] * own_rows(cot_low).astype(F32)
    upstream_other = weight_other[:, None] * other_rows(cot_low).astype(F32)
    upstream_low = jnp.concatenate([upstream, upstream_other], axis=0).astype(BF16)
    attn_out, upstream, upstream_low = lax.optimization_barrier((attn_out, upstream, upstream_low))
    residual = x_own.astype(F32) + attn_out + bias_p
    hat2, inverse2 = norm_stats(residual)
    ln2_own = (hat2 * gain2 + shift2).astype(BF16)
    ln2_low = jnp.concatenate([ln2_own, swap(ln2_own, "mp", 1)], axis=0)
    pre_act = dot_f32("td,df->tf", ln2_low, w_fc) + fc_bias_master[None]
    hidden_low = gelu_tanh(pre_act).astype(BF16)

    def scatter_product(product):
        return lax.psum_scatter(product, "dp", scatter_dimension=0, tiled=True)

    down_product = dot_f32("td,tf->df", upstream_low, hidden_low).astype(BF16)
    down_product, w_down = lax.optimization_barrier((down_product, w_down))
    down_reduced = scatter_product(down_product)

    back_act = dot_f32("td,df->tf", upstream_low, w_down)
    back_pre = (back_act * gelu_slope(pre_act)).astype(BF16)
    fc_bias_sum = jnp.sum(back_pre, axis=0, dtype=F32)
    fc_product = dot_f32("td,tf->df", ln2_low, back_pre).astype(BF16)

    back_ln2 = sum_over_cores(lambda rows: dot_f32("tf,df->td", rows, w_fc), back_pre)
    back_ln2 = sum_across(back_ln2)
    mlp_part = sum_over_cores(lambda rows: dot_f32("tf,df->td", rows, w_down), hidden_low)
    fc_product, mlp_part, back_ln2 = lax.optimization_barrier((fc_product, mlp_part, back_ln2))
    gain2_sum = jnp.sum(back_ln2 * hat2, axis=0)
    shift2_sum = jnp.sum(back_ln2, axis=0)
    back_resid = upstream + norm_back(back_ln2, hat2, inverse2, gain2)
    ga_own = back_resid.astype(BF16)
    ga_low = jnp.concatenate([ga_own, swap(ga_own, "mp", 1)], axis=0)
    back_mixed = dot_f32("td,de->te", ga_low, w_proj).astype(BF16)
    back_mixed = halves_swapped(back_mixed[:half], back_mixed[half:])
    back_qkv = jnp.concatenate(attend_back(qkv, back_mixed, seq_count, local_heads), axis=1)
    attn_bias_sum = jnp.sum(back_qkv, axis=0, dtype=F32).reshape(3, head_width)[0::2]
    back_qkv_local = halves_swapped(back_qkv[:half], back_qkv[half:])
    back_part = sum_over_cores(lambda rows: dot_f32("te,de->td", rows, w_qkv), back_qkv_local)
    qkv_part = dot_f32("td,te->de", ln1_low, back_qkv).astype(BF16)
    proj_part = dot_f32("td,te->de", ga_low, mixed_low).astype(BF16)
    total_tile = jnp.broadcast_to(valid_total, (8, 128))
    open_row = jnp.zeros_like(gain2_sum)
    norm_part = jnp.stack(
        [
            open_row,
            open_row,
            gain2_sum,
            shift2_sum,
            jnp.sum(back_resid, axis=0),
            jnp.sum(upstream, axis=0),
            open_row,
            open_row,
        ],
        axis=0,
    )
    norm_part = jnp.moveaxis(norm_part.reshape(8, dp_count, depth), 1, 0)
    bias_part = jnp.concatenate([attn_bias_sum.reshape(-1), fc_bias_sum]).reshape(-1, 128)
    (fc_raw, qkv_raw, proj_raw), square, norm_raw, bias_raw, whole, block_part = last_sums(
        [fc_product, qkv_part, proj_part],
        [back_part, mlp_part],
        x_own,
        back_resid,
        residual,
        total_tile,
        gain1,
        bias_d,
        norm_part,
        bias_part,
    )
    square = sum_everywhere(square, total_tile, [down_reduced], 3)
    grad_norm = jnp.sqrt(square[0, 0])
    bias_raw = bias_raw.reshape(-1)
    raw_grads = [
        norm_raw[:columns],
        bias_raw[: 2 * head_width].reshape(2, head_width),
        bias_raw[2 * head_width :].reshape(1, -1),
        qkv_raw,
        proj_raw,
        fc_raw,
        down_reduced,
    ]
    masters = (
        norm_master,
        attn_bias_master,
        qkv_master,
        proj_master,
        fc_bias_master,
        fc_master,
        down_master,
    )
    moments = (
        norm_moment,
        attn_bias_moment,
        qkv_moment,
        proj_moment,
        fc_bias_moment,
        fc_moment,
        down_moment,
    )
    averages = (
        norm_average,
        attn_bias_average,
        qkv_average,
        proj_average,
        fc_bias_average,
        fc_average,
        down_average,
    )
    order = (0, 1, 4, 2, 3, 5, 6)

    def arranged(values):
        values = [values[i] for i in order]
        values[0] = values[0].T
        values[2] = values[2].reshape(1, -1)
        values[3] = jnp.moveaxis(values[3], 1, 0)
        return values

    def returned(values):
        values = list(values)
        values[0] = values[0].T
        values[2] = values[2].reshape(-1)
        values[3] = jnp.moveaxis(values[3], 0, 1)
        return [values[order.index(i)] for i in range(7)]

    steps = step_all(
        square,
        total_tile,
        raw_grads,
        arranged(masters),
        arranged(moments),
        arranged(averages),
        3,
        6,
    )
    grads_out, momenta_out, averaged_out, updated_out, copies_out = map(returned, steps)
    return (
        block_part,
        whole,
        grads_out[0],
        grads_out[1],
        grads_out[2],
        grads_out[3],
        grads_out[4],
        grads_out[5],
        grads_out[6],
        momenta_out[0],
        momenta_out[1],
        momenta_out[2],
        momenta_out[3],
        momenta_out[4],
        momenta_out[5],
        momenta_out[6],
        averaged_out[0],
        averaged_out[1],
        averaged_out[2],
        averaged_out[3],
        averaged_out[4],
        averaged_out[5],
        averaged_out[6],
        updated_out[0],
        updated_out[1],
        updated_out[2],
        updated_out[3],
        updated_out[4],
        updated_out[5],
        updated_out[6],
        copies_out[0],
        copies_out[1],
        copies_out[2],
        copies_out[3],
        copies_out[4],
        copies_out[5],
        copies_out[6],
        grad_norm,
    )


def solution(mesh):
    placed = (
        P("dp", None),
        P("dp", None),
        P("dp"),
        P("dp", None),
        P(),
        P("dp", None),
        P(None, "mp"),
        P("dp", None, "mp"),
        P("dp", "mp"),
        P("mp"),
        P("dp", "mp"),
        P("dp", "mp"),
        P("dp", None),
        P(None, "mp"),
        P("dp", None, "mp"),
        P("dp", "mp"),
        P("mp"),
        P("dp", "mp"),
        P("dp", "mp"),
        P("dp", None),
        P(None, "mp"),
        P("dp", None, "mp"),
        P("dp", "mp"),
        P("mp"),
        P("dp", "mp"),
        P("dp", "mp"),
    )
    return jax.shard_map(
        local,
        mesh=mesh,
        in_specs=placed,
        out_specs=(
            P("dp", None),
            P("dp", None),
            P("dp", None),
            P(None, "mp"),
            P("dp", None, "mp"),
            P("dp", "mp"),
            P("mp"),
            P("dp", "mp"),
            P("dp", "mp"),
            P("dp", None),
            P(None, "mp"),
            P("dp", None, "mp"),
            P("dp", "mp"),
            P("mp"),
            P("dp", "mp"),
            P("dp", "mp"),
            P("dp", None),
            P(None, "mp"),
            P("dp", None, "mp"),
            P("dp", "mp"),
            P("mp"),
            P("dp", "mp"),
            P("dp", "mp"),
            P("dp", None),
            P(None, "mp"),
            P("dp", None, "mp"),
            P("dp", "mp"),
            P("mp"),
            P("dp", "mp"),
            P("dp", "mp"),
            P("dp", None),
            P(None, "mp"),
            P("dp", None, "mp"),
            P("dp", "mp"),
            P("mp"),
            P("dp", "mp"),
            P("dp", "mp"),
            P(),
        ),
        check_vma=False,
    )
```

```python
import functools
import math

import jax
import jax.numpy as jnp
from jax import lax
from jax.experimental import pallas as pl
from jax.experimental.pallas import tpu as pltpu
from jax.sharding import PartitionSpec as P

HEAD_DIM = 128
LEN = 1024


EPS = 1e-05
MOMENTUM = 0.9
RATE = 192.0
KEEP = 0.9
NEG = -1e30
BF16 = jnp.bfloat16
F32 = jnp.float32
MESH = pl.DeviceIdType.MESH


def dot_f32(eq, left, right):
    return jnp.einsum(eq, left, right, preferred_element_type=F32)


def swap(value, axis, flip):
    size = lax.axis_size(axis)
    return lax.ppermute(value, axis, [(i, i ^ flip) for i in range(size)])


def gather_kernel(outer, pieces, count, *refs):
    shards, wholes = refs[:count], refs[count : 2 * count]
    send, recv, local = refs[2 * count :]
    me = lax.axis_index("dp")
    out, side = me // 2, me % 2
    pair = out * 2 + 1 - side
    hops = outer - 1
    total = len(pieces)
    line = ((0, 1), (1, -1))

    def has(way, steps):
        return out >= steps if way > 0 else out + steps < outer

    def follows(way):
        return out + 1 < outer if way > 0 else out >= 1

    barrier = pltpu.get_barrier_semaphore()
    for peer in [lax.rem(out + r, outer) * 2 + side for r in range(1, outer)] + [pair]:
        pl.semaphore_signal(barrier, inc=1, device_id={"dp": peer}, device_id_type=MESH)
    pl.semaphore_wait(barrier, outer)

    def slot(p, device):
        a, plane, start, rows, _ = pieces[p]
        depth = shards[a].shape[-2]
        where = pl.ds(device * depth + start, rows)
        if plane is None:
            return wholes[a].at[where]
        width = shards[a].shape[-1]
        return wholes[a].at[where, pl.ds(plane * width, width)]

    def own(p):
        a, plane, start, rows, _ = pieces[p]
        where = pl.ds(start, rows)
        return shards[a].at[where] if plane is None else shards[a].at[plane, where]

    def remote(p, lane, source, target, peer):
        return pltpu.make_async_remote_copy(
            src_ref=source,
            dst_ref=target,
            send_sem=send.at[p, lane],
            recv_sem=recv.at[p, lane],
            device_id={"dp": peer},
            device_id_type=MESH,
        )

    def pass_on(p, other, index, way, steps):
        origin = (out - way * (steps - 1)) * 2 + (1 - side if other else side)
        here = slot(p, origin)
        source = own(p) if steps == 1 and not other else here
        lane = (2 * int(other) + index) * hops + steps - 1
        return remote(p, lane, source, here, (out + way) * 2 + side)

    def arrival(p, other, index, way, steps):
        origin = (out - way * steps) * 2 + (1 - side if other else side)
        lane = (2 * int(other) + index) * hops + steps - 1
        return remote(p, lane, slot(p, origin), slot(p, origin), pair)

    def to_pair(p, index, way, steps):
        if steps == 0:
            return remote(p, 4 * hops, own(p), slot(p, me), pair)
        here = slot(p, (out - way * steps) * 2 + side)
        return remote(p, (2 + index) * hops + steps - 1, here, here, pair)

    def begin(p):
        to_pair(p, 0, 1, 0).start()
        pltpu.make_async_copy(own(p), slot(p, me), local.at[p]).start()
        for index, way in line:

            @pl.when(follows(way))
            def _():
                pass_on(p, False, index, way, 1).start()

    def proceed(p, other, steps):
        early = pieces[p][4]
        for index, way in line:

            @pl.when(has(way, steps))
            def _():
                arrival(p, other, index, way, steps).wait_recv()
                if not early:
                    to_pair(p, index, way, steps).start()

            if steps < hops:

                @pl.when(jnp.logical_and(has(way, steps), follows(way)))
                def _():
                    pass_on(p, other, index, way, steps + 1).start()

    def cross(p):
        to_pair(p, 0, 1, 0).wait_recv()
        for index, way in line:

            @pl.when(follows(way))
            def _():
                pass_on(p, True, index, way, 1).start()

    lead = 4
    for p in range(min(lead, total)):
        begin(p)
    for wave in range(total + outer):
        if wave + lead < total:
            begin(wave + lead)
        if wave < total and pieces[wave][4]:
            cross(wave)
        for steps in range(1, outer):
            p = wave - steps + 1
            if 0 <= p < total:
                proceed(p, False, steps)
            p -= 1
            if 0 <= p < total and pieces[p][4]:
                proceed(p, True, steps)
    for p in range(total):
        early = pieces[p][4]
        to_pair(p, 0, 1, 0).wait_send()
        if not early:
            to_pair(p, 0, 1, 0).wait_recv()
        pltpu.make_async_copy(own(p), slot(p, me), local.at[p]).wait()
        for index, way in line:
            for other in (False, True) if early else (False,):
                for steps in range(1, outer):

                    @pl.when(jnp.logical_and(has(way, steps - 1), follows(way)))
                    def _():
                        pass_on(p, other, index, way, steps).wait_send()

            if not early:
                for steps in range(1, outer):

                    @pl.when(has(way, steps))
                    def _():
                        to_pair(p, index, way, steps).wait_send()
                        remote(
                            p,
                            (2 + index) * hops + steps - 1,
                            slot(p, me),
                            slot(p, (out - way * steps) * 2 + 1 - side),
                            pair,
                        ).wait_recv()


def gather_rows(shards, cuts, early, collective_id):
    size = lax.axis_size("dp")
    outer = size // 2
    count = len(shards)
    pieces, shapes = [], []
    for a, shard in enumerate(shards):
        depth, width = shard.shape[-2:]
        planes = [None] if shard.ndim == 2 else list(range(shard.shape[0]))
        rows = depth // cuts[a]
        for plane in planes:
            for i in range(cuts[a]):
                pieces.append((a, plane, i * rows, rows, len(pieces) in early))
        shapes.append(jax.ShapeDtypeStruct((size * depth, width * len(planes)), shard.dtype))
    anywhere = pl.BlockSpec(memory_space=pl.ANY)
    lanes = pltpu.SemaphoreType.DMA((len(pieces), 4 * outer - 3))
    return pl.pallas_call(
        functools.partial(gather_kernel, outer, pieces, count),
        out_shape=shapes,
        in_specs=[anywhere] * count,
        out_specs=[anywhere] * count,
        scratch_shapes=[lanes, lanes, pltpu.SemaphoreType.DMA((len(pieces),))],
        compiler_params=pltpu.CompilerParams(collective_id=collective_id, has_side_effects=True),
    )(*shards)


def remote_copy(source, target, send_sem, recv_sem, device):
    return pltpu.make_async_remote_copy(
        src_ref=source,
        dst_ref=target,
        send_sem=send_sem,
        recv_sem=recv_sem,
        device_id=device,
        device_id_type=MESH,
    )


def last_kernel(dp_count, mp_count, depth, pieces, count, tile_rows, *refs):
    refs = list(refs)

    def take(number):
        return [refs.pop(0) for _ in range(number)]

    grads = take(count)
    crossed = take(2)
    x_hbm, back_hbm, resid_hbm, total_ref, gain_ref, shift_ref, norm_ref, bias_ref = take(8)
    raws = take(count)
    square_ref, norm_out, bias_out, whole_out, block_out = take(5)
    bits = dp_count.bit_length() - 1
    own = take(count)
    got = [take(count) for _ in range(bits)]
    parts, taken = take(2), take(2)
    x_ref, back_ref, resid_ref, block_ref, sums, norm_own, norm_in, bias_in = take(8)
    half_send, half_recv, local, loading = take(4)
    cross_send, cross_recv, norm_send, norm_recv, bias_send, bias_recv = take(6)
    core_send, core_recv, placing = take(3)

    me, across = lax.axis_index("dp"), lax.axis_index("mp")
    mine = [me // (1 << bit) % 2 for bit in range(bits)]
    falling = list(reversed(range(bits)))
    core = across % 2
    near = across + 1 - 2 * core
    other = {"mp": lax.rem(across + 2, 4)}
    half = x_ref.shape[0]

    def spot(kd, flip):
        return {"dp": lax.rem(me + kd, dp_count), "mp": near if flip else across}

    hops = [(kd, flip) for kd in range(dp_count) for flip in range(2)][1:]
    barrier = pltpu.get_barrier_semaphore()
    for kd, flip in hops:
        pl.semaphore_signal(barrier, inc=1, device_id=spot(kd, flip), device_id_type=MESH)
    pl.semaphore_signal(barrier, inc=1, device_id=other, device_id_type=MESH)
    pl.semaphore_wait(barrier, len(hops) + 1)

    crosses = [
        remote_copy(crossed[i], taken[i], cross_send.at[i], cross_recv.at[i], other)
        for i in range(2)
    ]
    crosses[0].start()

    everything = slice(None)

    def first_index(p, value):
        return tuple(value if bit == pieces[p][3][0] else everything for bit in falling)

    def index(p, phase, value):
        order = pieces[p][3]
        place = []
        for bit in falling:
            if bit in order[1:phase]:
                place.append(mine[bit])
            elif phase and bit == order[phase]:
                place.append(value)
            elif bit != order[0]:
                place.append(everything)
        return tuple(place)

    def trade(p, phase):
        a, start, rows, order = pieces[p]
        bit, rows = order[phase], (pl.ds(start, rows),)
        if phase:
            source = own[a].at[index(p, phase, 1 - mine[bit]) + rows]
        else:
            source = grads[a].at[first_index(p, 1 - mine[bit]) + rows]
        return remote_copy(
            source,
            got[phase][a].at[(everything,) * (bits - 1 - phase) + rows],
            half_send.at[p, phase],
            half_recv.at[p, phase],
            {"dp": me + (1 - 2 * mine[bit]) * (1 << bit)},
        )

    def load(p):
        a, start, rows, order = pieces[p]
        rows = (pl.ds(start, rows),)
        return pltpu.make_async_copy(
            grads[a].at[first_index(p, mine[order[0]]) + rows],
            own[a].at[(everything,) * (bits - 1) + rows],
            local.at[p],
        )

    lead, skew = 12, 4
    for p in range(min(lead, len(pieces))):
        trade(p, 0).start()
    for p in range(len(pieces)):
        load(p).start()
    later = [
        pltpu.make_async_copy(source, target, loading.at[i])
        for i, (source, target) in enumerate(
            [
                (crossed[0], parts[0]),
                (crossed[1], parts[1]),
                (x_hbm, x_ref),
                (back_hbm, back_ref),
                (resid_hbm, resid_ref),
            ]
        )
    ]
    for copy in later:
        copy.start()
    norm_own[...] = norm_ref[...]
    bias_in[me] = bias_ref[...]
    bias_copies = [
        remote_copy(bias_ref, bias_in.at[me], bias_send.at[kd], bias_recv.at[kd], spot(kd, 0))
        for kd in range(1, dp_count)
    ]
    for copy in bias_copies:
        copy.start()
    total = total_ref[0:1, 0:1]
    squares = []

    def finish(p, phase):
        a, start, rows, order = pieces[p]
        rows = (pl.ds(start, rows),)
        if phase == 0:
            load(p).wait()
        trade(p, phase).wait_recv()
        if phase == 0 and p + lead < len(pieces):
            trade(p + lead, 0).start()
        kept = index(p, phase, mine[order[phase]]) + rows
        both = own[a][kept].astype(F32)
        both = both + got[phase][a][(everything,) * (bits - 1 - phase) + rows].astype(F32)
        if phase < bits - 1:
            own[a][kept] = both.astype(BF16)
            trade(p, phase + 1).start()
        else:
            raw = both / total
            raws[a][rows] = raw
            squares.append(jnp.sum(raw * raw, keepdims=True))

    waves = len(pieces) + skew * (bits - 1)

    def advance(first, last):
        for wave in range(first, last):
            for phase in range(bits):
                if 0 <= wave - skew * phase < len(pieces):
                    finish(wave - skew * phase, phase)

    middle, later_on = 2 * waves // 5, 4 * waves // 5
    advance(0, middle)

    for copy in later:
        copy.wait()
    crosses[0].wait_recv()
    crosses[1].start()
    sums[...] = jnp.zeros_like(sums)
    gain = gain_ref[0:1]

    @pl.loop(0, half // tile_rows)
    def _(i):
        where = pl.ds(pl.multiple_of(i * tile_rows, tile_rows), tile_rows)
        hat, inverse = norm_stats(x_ref[where].astype(F32))
        back = parts[0][where].astype(F32) + taken[0][where].astype(F32)
        product = back * hat
        sums[0] += jnp.sum(product.reshape(tile_rows // 8, 8, -1), axis=0)
        sums[1] += jnp.sum(back.reshape(tile_rows // 8, 8, -1), axis=0)
        back_ref[where] = back_ref[where] + norm_back(back, hat, inverse, gain)

    whole_place = pl.ds(pl.multiple_of(core * half, half), half)
    whole_copy = remote_copy(
        back_ref, whole_out.at[whole_place], core_send.at[0], core_recv.at[0], spot(0, 1)
    )
    whole_copy.start()
    whole_local = pltpu.make_async_copy(back_ref, whole_out.at[whole_place], placing.at[0])
    whole_local.start()
    for k in range(2):
        row = jnp.sum(sums[k], axis=0, keepdims=True)
        for d in range(dp_count):
            norm_own[d, k : k + 1] = row[:, d * depth : (d + 1) * depth]
    norm_copies = [
        remote_copy(
            norm_own.at[lax.rem(me + kd, dp_count)],
            norm_in.at[me * 2 + core],
            norm_send.at[kd, flip],
            norm_recv.at[kd, flip],
            spot(kd, flip),
        )
        for kd, flip in hops
    ]
    for copy in norm_copies:
        copy.start()
    norm_in[me * 2 + core] = norm_own[me]

    advance(middle, later_on)

    crosses[1].wait_recv()
    shift = shift_ref[0:1]

    @pl.loop(0, half // tile_rows)
    def _(i):
        where = pl.ds(pl.multiple_of(i * tile_rows, tile_rows), tile_rows)
        mlp = parts[1][where].astype(F32) + taken[1][where].astype(F32)
        block_ref[where] = (resid_ref[where] + mlp + shift).astype(BF16)

    block_copy = remote_copy(
        block_ref, block_out.at[whole_place], core_send.at[1], core_recv.at[1], spot(0, 1)
    )
    block_copy.start()
    block_local = pltpu.make_async_copy(block_ref, block_out.at[whole_place], placing.at[1])
    block_local.start()
    advance(later_on, waves)

    for copy in norm_copies + bias_copies:
        copy.wait_recv()
    norm = norm_in[0]
    for i in range(1, 2 * dp_count):
        norm = norm + norm_in[i]
    bias = bias_in[0]
    for i in range(1, dp_count):
        bias = bias + bias_in[i]
    norm = norm / total
    bias = bias / total
    norm_out[...] = norm
    bias_out[...] = bias
    square = jnp.sum(norm * norm, keepdims=True) / float(mp_count)
    square = square + jnp.sum(bias * bias, keepdims=True) / float(dp_count)

    for part in squares:
        square = square + part
    square_ref[...] = jnp.broadcast_to(square, square_ref.shape)
    for p in range(len(pieces)):
        for phase in range(bits):
            trade(p, phase).wait_send()
    for copy in crosses + norm_copies + bias_copies:
        copy.wait_send()
    whole_copy.wait()
    whole_local.wait()
    block_copy.wait()
    block_local.wait()


def last_sums(grads, crossed, x_own, back, residual, total, gain, shift, norm_part, bias_part):
    dp_count, mp_count = lax.axis_size("dp"), lax.axis_size("mp")
    bits = dp_count.bit_length() - 1
    count, depth = len(grads), grads[0].shape[0] // dp_count
    half, width = x_own.shape
    straight = list(range(bits))
    turned = [1, 0] + straight[2:]
    pieces = []
    for a, grad in enumerate(grads):
        rows = max(16, depth * 256 // grad.shape[1] // 4)
        rows = min(rows // 16 * 16, depth)
        number = depth // rows
        for i in range(number):
            order = turned if a == 0 and i % 2 == 0 else straight
            pieces.append(((2 * i + 1) / number, (a, i * rows, rows, order)))
    pieces = [piece for _, piece in sorted(pieces, key=lambda piece: piece[0])]
    anywhere = pl.BlockSpec(memory_space=pl.ANY)
    inside = pl.BlockSpec(memory_space=pltpu.VMEM)

    def blocks(number):
        return [pltpu.VMEM((2,) * number + (depth, grad.shape[1]), BF16) for grad in grads]

    slim, wide = pltpu.VMEM((half, width), BF16), pltpu.VMEM((half, width), F32)
    dma = pltpu.SemaphoreType.DMA
    results = pl.pallas_call(
        functools.partial(last_kernel, dp_count, mp_count, depth, pieces, count, min(64, half)),
        out_shape=[jax.ShapeDtypeStruct((depth, grad.shape[1]), F32) for grad in grads]
        + [
            jax.ShapeDtypeStruct((8, 128), F32),
            jax.ShapeDtypeStruct(norm_part.shape[1:], F32),
            jax.ShapeDtypeStruct(bias_part.shape, F32),
            jax.ShapeDtypeStruct((2 * half, width), F32),
            jax.ShapeDtypeStruct((2 * half, width), BF16),
        ],
        in_specs=[anywhere] * (count + 5) + [inside] * 5,
        out_specs=[inside] * (count + 3) + [anywhere] * 2,
        scratch_shapes=blocks(bits - 1)
        + sum([blocks(bits - 1 - phase) for phase in range(bits)], [])
        + [slim] * 4
        + [slim, wide, wide, slim]
        + [
            pltpu.VMEM((2, 8, width), F32),
            pltpu.VMEM(norm_part.shape, F32),
            pltpu.VMEM((2 * dp_count, *norm_part.shape[1:]), F32),
            pltpu.VMEM((dp_count, *bias_part.shape), F32),
        ]
        + [dma((len(pieces), bits))] * 2
        + [dma((len(pieces),)), dma((5,))]
        + [dma((2,))] * 2
        + [dma((dp_count, 2))] * 2
        + [dma((dp_count,))] * 2
        + [dma((2,))] * 3,
        compiler_params=pltpu.CompilerParams(
            collective_id=1, has_side_effects=True, vmem_limit_bytes=58 << 20
        ),
    )(
        *[grad.reshape((2,) * bits + (depth, -1)) for grad in grads],
        *crossed,
        x_own,
        back,
        residual,
        total,
        gain,
        shift,
        norm_part,
        bias_part,
    )
    return results[:count], *results[count:]


def everyone(dp_count, mp_count):
    return [(kd, km) for kd in range(dp_count) for km in range(mp_count)][1:]


def square_kernel(dp_count, mp_count, count, tile_ref, total_ref, *refs):
    summed, (out_ref, tiles, own_ref, send, recv) = refs[:count], refs[count:]
    me, across = lax.axis_index("dp"), lax.axis_index("mp")
    hops = everyone(dp_count, mp_count)

    def spot(kd, km):
        return {"dp": lax.rem(me + kd, dp_count), "mp": lax.rem(across + km, mp_count)}

    barrier = pltpu.get_barrier_semaphore()
    for kd, km in hops:
        pl.semaphore_signal(barrier, inc=1, device_id=spot(kd, km), device_id_type=MESH)
    total = total_ref[0:1, 0:1]
    square = tile_ref[...]
    for ref in summed:
        raw = ref[...].astype(F32) / total
        square = square + jnp.sum(raw * raw)
    own_ref[...] = square
    pl.semaphore_wait(barrier, len(hops))
    slot = me * mp_count + across
    copies = [
        remote_copy(own_ref, tiles.at[slot], send.at[i], recv.at[i], spot(kd, km))
        for i, (kd, km) in enumerate(hops)
    ]
    for copy in copies:
        copy.start()
    tiles[slot] = own_ref[...]
    for copy in copies:
        copy.wait_recv()
    square = tiles[0]
    for i in range(1, dp_count * mp_count):
        square = square + tiles[i]
    out_ref[...] = square
    for copy in copies:
        copy.wait_send()


def sum_everywhere(tile, total, summed, collective_id):
    dp_count, mp_count = lax.axis_size("dp"), lax.axis_size("mp")
    inside = pl.BlockSpec(memory_space=pltpu.VMEM)
    hops = pltpu.SemaphoreType.DMA((dp_count * mp_count - 1,))
    return pl.pallas_call(
        functools.partial(square_kernel, dp_count, mp_count, len(summed)),
        out_shape=jax.ShapeDtypeStruct(tile.shape, F32),
        in_specs=[inside] * (2 + len(summed)),
        out_specs=inside,
        scratch_shapes=[
            pltpu.VMEM((dp_count * mp_count, *tile.shape), F32),
            pltpu.VMEM(tile.shape, F32),
            hops,
            hops,
        ],
        compiler_params=pltpu.CompilerParams(
            collective_id=collective_id, has_side_effects=True, vmem_limit_bytes=16 << 20
        ),
    )(tile, total, *summed)


def step_kernel(splits, divided, whole_count, square_ref, total_ref, *refs):
    count = len(splits)
    refs = list(refs)
    raws = [[refs.pop(0) for _ in range(number)] for number in splits]
    masters, moments, averages = [refs[i * count : (i + 1) * count] for i in range(3)]
    outs = [refs[(3 + i) * count : (4 + i) * count] for i in range(5)]
    clip = jnp.minimum(1.0, 1.0 / (jnp.sqrt(square_ref[0:1, 0:1]) + 1e-06))
    total = total_ref[0:1, 0:1]

    def update(raw, master, moment, average):
        clipped = raw * clip
        momentum = MOMENTUM * moment + clipped
        updated = master - RATE * (clipped + MOMENTUM * momentum)
        averaged = KEEP * average + (1.0 - KEEP) * updated
        return clipped, momentum, averaged, updated, updated.astype(BF16)

    def apply(a):
        if len(masters[a].shape) == 2:
            raw = [part[...].astype(F32) for part in raws[a]]
            raw = raw[0] if len(raw) == 1 else jnp.concatenate(raw, axis=1)
            if a >= divided:
                raw = raw / total
            results = update(raw, masters[a][...], moments[a][...], averages[a][...])
            for out, result in zip(outs, results):
                out[a][...] = result
        else:
            width = masters[a].shape[2]
            for c in range(masters[a].shape[0]):
                results = update(
                    raws[a][0][:, c * width : (c + 1) * width],
                    masters[a][c],
                    moments[a][c],
                    averages[a][c],
                )
                for out, result in zip(outs, results):
                    out[a][c] = result

    for a in range(whole_count, count):
        apply(a)

    @pl.when(pl.program_id(0) == 0)
    def _():
        for a in range(whole_count):
            apply(a)


def step_all(square, total, raws, masters, moments, averages, whole_count, divided):
    raws = [raw if isinstance(raw, tuple) else (raw,) for raw in raws]
    depth = raws[-1][0].shape[0]
    rows = min(32, depth)

    def spec(value, a):
        shape = value.shape
        if a < whole_count:
            return pl.BlockSpec(shape, lambda i, n=len(shape): (0,) * n)
        if len(shape) == 3:
            return pl.BlockSpec((shape[0], rows, shape[2]), lambda i: (0, i, 0))
        return pl.BlockSpec((rows, shape[1]), lambda i: (i, 0))

    def specs(values):
        return [spec(value, a) for a, value in enumerate(values)]

    tile = pl.BlockSpec((8, 128), lambda i: (0, 0))
    wide = [jax.ShapeDtypeStruct(master.shape, F32) for master in masters]
    slim = [jax.ShapeDtypeStruct(master.shape, BF16) for master in masters]
    results = pl.pallas_call(
        functools.partial(step_kernel, [len(raw) for raw in raws], divided, whole_count),
        grid=(depth // rows,),
        out_shape=wide * 4 + slim,
        in_specs=[tile, tile]
        + [spec(part, a) for a, raw in enumerate(raws) for part in raw]
        + specs(masters) * 3,
        out_specs=specs(masters) * 5,
        compiler_params=pltpu.CompilerParams(vmem_limit_bytes=56 << 20),
    )(square, total, *sum(raws, ()), *masters, *moments, *averages)
    count = len(masters)
    return [results[i * count : (i + 1) * count] for i in range(5)]


def score_block(query_ref, key_ref, first, rows, scale):
    width = first + rows
    scores = scale * lax.dot_general(
        query_ref[first:width], key_ref[:width], (((1,), (1,)), ((), ())), preferred_element_type=F32
    )
    row = first + lax.broadcasted_iota(jnp.int32, (rows, width), 0)
    column = lax.broadcasted_iota(jnp.int32, (rows, width), 1)
    scores = jnp.where(column <= row, scores, NEG)
    raised = jnp.exp(scores - jnp.max(scores, axis=-1, keepdims=True))
    return raised / jnp.sum(raised, axis=-1, keepdims=True)


def attend_kernel(rows, scale, query_ref, key_ref, value_ref, out_ref):
    for first in range(0, query_ref.shape[0], rows):
        prob = score_block(query_ref, key_ref, first, rows, scale)
        out_ref[first : first + rows] = jnp.dot(
            prob.astype(BF16), value_ref[: first + rows], preferred_element_type=F32
        ).astype(BF16)


def attend_back_kernel(
    rows, scale, query_ref, key_ref, value_ref, back_ref, gq_ref, gk_ref, gv_ref, key_sum, value_sum
):
    key_sum[...] = jnp.zeros_like(key_sum)
    value_sum[...] = jnp.zeros_like(value_sum)
    over_rows = (((0,), (0,)), ((), ()))
    for first in range(0, query_ref.shape[0], rows):
        width = first + rows
        prob = score_block(query_ref, key_ref, first, rows, scale)
        back = back_ref[first:width]
        back_prob = lax.dot_general(
            back, value_ref[:width], (((1,), (1,)), ((), ())), preferred_element_type=F32
        )
        value_sum[:width] += lax.dot_general(
            prob.astype(BF16), back, over_rows, preferred_element_type=F32
        )
        slope = jnp.sum(prob * back_prob, axis=-1, keepdims=True)
        back_score = (prob * (back_prob - slope)).astype(BF16)
        gq_ref[first:width] = (
            scale * jnp.dot(back_score, key_ref[:width], preferred_element_type=F32)
        ).astype(BF16)
        key_sum[:width] += lax.dot_general(
            back_score, query_ref[first:width], over_rows, preferred_element_type=F32
        )
    gk_ref[...] = (scale * key_sum[...]).astype(BF16)
    gv_ref[...] = value_sum[...].astype(BF16)


def attend(qkv, seq_count, heads):
    seq_len = qkv.shape[0] // seq_count
    rows = min(256, seq_len)
    columns = [
        pl.BlockSpec((seq_len, HEAD_DIM), lambda i, h, part=part: (i, part * heads + h))
        for part in range(3)
    ]
    return pl.pallas_call(
        functools.partial(attend_kernel, rows, 1.0 / math.sqrt(HEAD_DIM)),
        grid=(seq_count, heads),
        out_shape=jax.ShapeDtypeStruct((qkv.shape[0], heads * HEAD_DIM), BF16),
        in_specs=columns,
        out_specs=columns[0],
        compiler_params=pltpu.CompilerParams(vmem_limit_bytes=48 << 20),
    )(qkv, qkv, qkv)


def attend_back(qkv, back, seq_count, heads):
    seq_len = qkv.shape[0] // seq_count
    rows = min(256, seq_len)
    columns = [
        pl.BlockSpec((seq_len, HEAD_DIM), lambda i, h, part=part: (i, part * heads + h))
        for part in range(3)
    ]
    grads = jax.ShapeDtypeStruct((qkv.shape[0], heads * HEAD_DIM), BF16)
    return pl.pallas_call(
        functools.partial(attend_back_kernel, rows, 1.0 / math.sqrt(HEAD_DIM)),
        grid=(seq_count, heads),
        out_shape=[grads] * 3,
        in_specs=columns + columns[:1],
        out_specs=columns[:1] * 3,
        scratch_shapes=[pltpu.VMEM((seq_len, HEAD_DIM), F32)] * 2,
        compiler_params=pltpu.CompilerParams(vmem_limit_bytes=48 << 20),
    )(qkv, qkv, qkv, back)


def norm_stats(value):
    centre = jnp.mean(value, axis=-1, keepdims=True)
    centred = value - centre
    spread = jnp.mean(centred * centred, axis=-1, keepdims=True)
    inverse = lax.rsqrt(spread + EPS)
    return centred * inverse, inverse


def norm_back(back, hat, inverse, gain):
    scaled = back * gain
    mean = jnp.mean(scaled, axis=-1, keepdims=True)
    slope = jnp.mean(scaled * hat, axis=-1, keepdims=True)
    return inverse * (scaled - mean - hat * slope)


def gelu_parts(value):
    inner = 0.7978845608028654 * (value + 0.044715 * value * value * value)
    return jnp.tanh(inner)


def gelu_tanh(value):
    return 0.5 * value * (1.0 + gelu_parts(value))


def gelu_slope(value):
    tanh = gelu_parts(value)
    rise = 0.7978845608028654 * (1.0 + 3.0 * 0.044715 * value * value)
    return 0.5 * (1.0 + tanh) + 0.5 * value * (1.0 - tanh * tanh) * rise


def local(
    tokens,
    out_cot,
    lengths,
    seq_family,
    family_tokens,
    norm_master,
    attn_bias_master,
    qkv_master,
    proj_master,
    fc_bias_master,
    fc_master,
    down_master,
    norm_moment,
    attn_bias_moment,
    qkv_moment,
    proj_moment,
    fc_bias_moment,
    fc_moment,
    down_moment,
    norm_average,
    attn_bias_average,
    qkv_average,
    proj_average,
    fc_bias_average,
    fc_average,
    down_average,
):
    seq_count = lengths.shape[0]
    row_count = tokens.shape[0]
    seq_len = row_count // seq_count
    family_count = family_tokens.shape[0]
    depth, _, head_width = qkv_master.shape
    local_heads = head_width // HEAD_DIM
    mp_count = lax.axis_size("mp")
    dp_count = lax.axis_size("dp")
    outer = dp_count // 2
    place = lax.axis_index("dp")
    place_out, place_in = place // 2, place % 2
    side = lax.axis_index("mp") % 2
    half = row_count // 2

    def own_rows(value):
        return lax.dynamic_slice_in_dim(value, side * half, half, 0)

    def other_rows(value):
        return lax.dynamic_slice_in_dim(value, (1 - side) * half, half, 0)

    def halves_swapped(own, other):
        return jnp.where(
            side == 0,
            jnp.concatenate([own, other], axis=0),
            jnp.concatenate([other, own], axis=0),
        )

    columns = norm_master.shape[1]
    low_norm = jnp.pad(norm_master.astype(BF16).T, ((0, 16 - columns), (0, 0)))
    low_qkv = jnp.moveaxis(qkv_master, 1, 0).astype(BF16)
    low_proj = proj_master.astype(BF16)
    low_fc = fc_master.astype(BF16)
    low_down = down_master.astype(BF16)

    family_ids = jnp.arange(family_count, dtype=jnp.int32)
    member = seq_family == family_ids[None, :]
    local_counts = jnp.sum(jnp.where(member, lengths[:, None], 0), axis=0).astype(F32)
    count_tile = jnp.broadcast_to(jnp.pad(local_counts, (0, 128 - family_count))[None], (8, 128))
    w_norm, all_counts, w_qkv, w_proj, w_fc = gather_rows(
        [low_norm, count_tile, low_qkv, low_proj, low_fc], (1, 1, 2, 2, 8), (3, 8, 13), 0
    )
    w_norm = jnp.moveaxis(w_norm.reshape(dp_count, 16, depth), 0, 1).reshape(16, dp_count * depth)
    counts = jnp.sum(all_counts.reshape(dp_count, 8, 128)[:, 0], axis=0)[:family_count]
    low_down, w_fc = lax.optimization_barrier((low_down, w_fc))
    w_down = lax.all_gather(low_down, "dp", axis=0, tiled=True)

    valid_total = jnp.sum(counts)
    share = family_tokens.astype(F32) / jnp.sum(family_tokens).astype(F32)
    family_weight = share * valid_total / jnp.maximum(counts, float(LEN // 2))
    seq_weight = jnp.sum(jnp.where(member, family_weight[None, :], 0.0), axis=1)
    places = jnp.arange(seq_len, dtype=jnp.int32)
    token_weight = jnp.where(places[None, :] < lengths[:, None], seq_weight[:, None], 0.0).reshape(
        row_count
    )

    norm_full = w_norm.astype(F32)
    gain1, shift1, gain2, shift2, bias_p, bias_d = [norm_full[i][None] for i in range(6)]
    bias_row = jnp.concatenate(
        [attn_bias_master[0], jnp.zeros_like(attn_bias_master[0]), attn_bias_master[1]], axis=0
    )
    x_low = tokens
    cot_low = out_cot

    x_hat, _ = norm_stats(x_low.astype(F32))
    ln1_low = (x_hat * gain1 + shift1).astype(BF16)
    qkv = (dot_f32("td,de->te", ln1_low, w_qkv) + bias_row[None]).astype(BF16)
    mixed_low = attend(qkv, seq_count, local_heads)
    mixed_low = halves_swapped(mixed_low[:half], mixed_low[half:])

    def sum_over_cores(product, left):
        other = swap(product(left[half:]).astype(BF16), "mp", 1)
        return (product(left[:half]) + other.astype(F32)).astype(BF16)

    def sum_over_mp(product, left):
        return sum_across(sum_over_cores(product, left))

    def sum_across(part):
        flip = 2
        while flip < mp_count:
            part = part.astype(F32) + swap(part, "mp", flip).astype(F32)
            flip *= 2
            if flip < mp_count:
                part = part.astype(BF16)
        return part.astype(F32)

    x_own = own_rows(x_low)
    attn_out = sum_over_mp(lambda rows: dot_f32("te,de->td", rows, w_proj), mixed_low)
    weight_own, weight_other = own_rows(token_weight), other_rows(token_weight)
    upstream = weight_own[:, None] * own_rows(cot_low).astype(F32)
    upstream_other = weight_other[:, None] * other_rows(cot_low).astype(F32)
    upstream_low = jnp.concatenate([upstream, upstream_other], axis=0).astype(BF16)
    attn_out, upstream, upstream_low = lax.optimization_barrier((attn_out, upstream, upstream_low))
    residual = x_own.astype(F32) + attn_out + bias_p
    hat2, inverse2 = norm_stats(residual)
    ln2_own = (hat2 * gain2 + shift2).astype(BF16)
    ln2_low = jnp.concatenate([ln2_own, swap(ln2_own, "mp", 1)], axis=0)
    pre_act = dot_f32("td,df->tf", ln2_low, w_fc) + fc_bias_master[None]
    hidden_low = gelu_tanh(pre_act).astype(BF16)

    def scatter_product(product):
        return lax.psum_scatter(product, "dp", scatter_dimension=0, tiled=True)

    down_product = dot_f32("td,tf->df", upstream_low, hidden_low).astype(BF16)
    down_product, w_down = lax.optimization_barrier((down_product, w_down))
    down_reduced = scatter_product(down_product)

    back_act = dot_f32("td,df->tf", upstream_low, w_down)
    back_pre = (back_act * gelu_slope(pre_act)).astype(BF16)
    fc_bias_sum = jnp.sum(back_pre, axis=0, dtype=F32)
    fc_product = dot_f32("td,tf->df", ln2_low, back_pre).astype(BF16)

    back_ln2 = sum_over_cores(lambda rows: dot_f32("tf,df->td", rows, w_fc), back_pre)
    back_ln2 = sum_across(back_ln2)
    mlp_part = sum_over_cores(lambda rows: dot_f32("tf,df->td", rows, w_down), hidden_low)
    fc_product, mlp_part, back_ln2 = lax.optimization_barrier((fc_product, mlp_part, back_ln2))
    gain2_sum = jnp.sum(back_ln2 * hat2, axis=0)
    shift2_sum = jnp.sum(back_ln2, axis=0)
    back_resid = upstream + norm_back(back_ln2, hat2, inverse2, gain2)
    ga_own = back_resid.astype(BF16)
    ga_low = jnp.concatenate([ga_own, swap(ga_own, "mp", 1)], axis=0)
    back_mixed = dot_f32("td,de->te", ga_low, w_proj).astype(BF16)
    back_mixed = halves_swapped(back_mixed[:half], back_mixed[half:])
    back_qkv = jnp.concatenate(attend_back(qkv, back_mixed, seq_count, local_heads), axis=1)
    attn_bias_sum = jnp.sum(back_qkv, axis=0, dtype=F32).reshape(3, head_width)[0::2]
    back_qkv_local = halves_swapped(back_qkv[:half], back_qkv[half:])
    back_part = sum_over_cores(lambda rows: dot_f32("te,de->td", rows, w_qkv), back_qkv_local)
    qkv_part = dot_f32("td,te->de", ln1_low, back_qkv).astype(BF16)
    proj_part = dot_f32("td,te->de", ga_low, mixed_low).astype(BF16)
    total_tile = jnp.broadcast_to(valid_total, (8, 128))
    open_row = jnp.zeros_like(gain2_sum)
    norm_part = jnp.stack(
        [
            open_row,
            open_row,
            gain2_sum,
            shift2_sum,
            jnp.sum(back_resid, axis=0),
            jnp.sum(upstream, axis=0),
            open_row,
            open_row,
        ],
        axis=0,
    )
    norm_part = jnp.moveaxis(norm_part.reshape(8, dp_count, depth), 1, 0)
    bias_part = jnp.concatenate([attn_bias_sum.reshape(-1), fc_bias_sum]).reshape(-1, 128)
    (fc_raw, qkv_raw, proj_raw), square, norm_raw, bias_raw, whole, block_part = last_sums(
        [fc_product, qkv_part, proj_part],
        [back_part, mlp_part],
        x_own,
        back_resid,
        residual,
        total_tile,
        gain1,
        bias_d,
        norm_part,
        bias_part,
    )
    square = sum_everywhere(square, total_tile, [down_reduced], 3)
    grad_norm = jnp.sqrt(square[0, 0])
    bias_raw = bias_raw.reshape(-1)
    raw_grads = [
        norm_raw[:columns],
        bias_raw[: 2 * head_width].reshape(2, head_width),
        bias_raw[2 * head_width :].reshape(1, -1),
        qkv_raw,
        proj_raw,
        fc_raw,
        down_reduced,
    ]
    masters = (
        norm_master,
        attn_bias_master,
        qkv_master,
        proj_master,
        fc_bias_master,
        fc_master,
        down_master,
    )
    moments = (
        norm_moment,
        attn_bias_moment,
        qkv_moment,
        proj_moment,
        fc_bias_moment,
        fc_moment,
        down_moment,
    )
    averages = (
        norm_average,
        attn_bias_average,
        qkv_average,
        proj_average,
        fc_bias_average,
        fc_average,
        down_average,
    )
    order = (0, 1, 4, 2, 3, 5, 6)

    def arranged(values):
        values = [values[i] for i in order]
        values[0] = values[0].T
        values[2] = values[2].reshape(1, -1)
        values[3] = jnp.moveaxis(values[3], 1, 0)
        return values

    def returned(values):
        values = list(values)
        values[0] = values[0].T
        values[2] = values[2].reshape(-1)
        values[3] = jnp.moveaxis(values[3], 0, 1)
        return [values[order.index(i)] for i in range(7)]

    steps = step_all(
        square,
        total_tile,
        raw_grads,
        arranged(masters),
        arranged(moments),
        arranged(averages),
        3,
        6,
    )
    grads_out, momenta_out, averaged_out, updated_out, copies_out = map(returned, steps)
    return (
        block_part,
        whole,
        grads_out[0],
        grads_out[1],
        grads_out[2],
        grads_out[3],
        grads_out[4],
        grads_out[5],
        grads_out[6],
        momenta_out[0],
        momenta_out[1],
        momenta_out[2],
        momenta_out[3],
        momenta_out[4],
        momenta_out[5],
        momenta_out[6],
        averaged_out[0],
        averaged_out[1],
        averaged_out[2],
        averaged_out[3],
        averaged_out[4],
        averaged_out[5],
        averaged_out[6],
        updated_out[0],
        updated_out[1],
        updated_out[2],
        updated_out[3],
        updated_out[4],
        updated_out[5],
        updated_out[6],
        copies_out[0],
        copies_out[1],
        copies_out[2],
        copies_out[3],
        copies_out[4],
        copies_out[5],
        copies_out[6],
        grad_norm,
    )


def solution(mesh):
    placed = (
        P("dp", None),
        P("dp", None),
        P("dp"),
        P("dp", None),
        P(),
        P("dp", None),
        P(None, "mp"),
        P("dp", None, "mp"),
        P("dp", "mp"),
        P("mp"),
        P("dp", "mp"),
        P("dp", "mp"),
        P("dp", None),
        P(None, "mp"),
        P("dp", None, "mp"),
        P("dp", "mp"),
        P("mp"),
        P("dp", "mp"),
        P("dp", "mp"),
        P("dp", None),
        P(None, "mp"),
        P("dp", None, "mp"),
        P("dp", "mp"),
        P("mp"),
        P("dp", "mp"),
        P("dp", "mp"),
    )
    return jax.shard_map(
        local,
        mesh=mesh,
        in_specs=placed,
        out_specs=(
            P("dp", None),
            P("dp", None),
            P("dp", None),
            P(None, "mp"),
            P("dp", None, "mp"),
            P("dp", "mp"),
            P("mp"),
            P("dp", "mp"),
            P("dp", "mp"),
            P("dp", None),
            P(None, "mp"),
            P("dp", None, "mp"),
            P("dp", "mp"),
            P("mp"),
            P("dp", "mp"),
            P("dp", "mp"),
            P("dp", None),
            P(None, "mp"),
            P("dp", None, "mp"),
            P("dp", "mp"),
            P("mp"),
            P("dp", "mp"),
            P("dp", "mp"),
            P("dp", None),
            P(None, "mp"),
            P("dp", None, "mp"),
            P("dp", "mp"),
            P("mp"),
            P("dp", "mp"),
            P("dp", "mp"),
            P("dp", None),
            P(None, "mp"),
            P("dp", None, "mp"),
            P("dp", "mp"),
            P("mp"),
            P("dp", "mp"),
            P("dp", "mp"),
            P(),
        ),
        check_vma=False,
    )
```
